256 devices in a mesh: dp: 32 (over z, x), mp: 8 (over y, core).
Axes of the slice: x: 4, y: 4, z: 8, core: 2. Of those that a mesh axis runs over, the one named last changes fastest.
Arguments:
- query: bfloat16 [8192, 4096], P('dp', 'mp'), may hold values from -400 to 400
- keys_values: bfloat16 [2, 8192, 512], P(None, 'dp'), may hold values from -6 to 6
- ancestors: int32 [64, 12], P('dp'), may hold values from -1 to 63, as said below
- tile_of_slot: int32 [64], replicated, may hold values from 0 to 63, as said below
- residual: bfloat16 [8192, 8192], P('dp', 'mp'), may hold values from -6 to 6
- norm_gain: float32 [8192], P('mp'), may hold values from 0.25 to 1.75
- out_weight: bfloat16 [4096, 8192], P('mp'), may hold values from -0.09375 to 0.09375
Outputs:
- hidden_out: bfloat16 [8192, 8192], P('dp', 'mp')
- normed: bfloat16 [8192, 8192], P('dp', 'mp')
The draws below stay inside these ranges and needn't reach their ends.
Inputs may be any that keep to these rules, and one draw needn't show every extreme that they name: Ids of tiles, or -1. Over all query tiles of one device's 2 positions, the ancestors that lie at the positions of any one device number at most 1 distinct tiles; some device reaches 1 in every draw. `tile_of_slot`: a permutation of the tile ids.
All inputs are finite; a program needn't handle non-finite values.
Results may differ from the reference program's by a relative error of at most 0.008.
Values may be sent and summed in bfloat16 or wider, within the bound.
No kernel may reach another device: no remote copies, remote signals or barrier semaphores. Data moves between devices by JAX's collectives and lax.ppermute only.
A program may use at most 64 MiB of HBM per device.

```python
import jax
import jax.numpy as jnp
from jax import lax

D = 8192
HEADS = 32
KV_HEADS = 4
HEAD = 128
TILE = 128
ANC = 12
TILES_DEV = 2
TILES = 64
TOKENS = 8192
N_MP = 8


def attention_inputs(key):
    queries = jax.random.normal(jax.random.fold_in(key, 201), (TOKENS, HEADS, HEAD), jnp.float32)
    pairs = jax.random.normal(jax.random.fold_in(key, 202), (2, TOKENS, KV_HEADS, HEAD), jnp.float32)
    queries = jnp.clip(queries, -6.0, 6.0)
    pairs = jnp.clip(pairs, -6.0, 6.0)
    return (queries.reshape(TOKENS, HEADS * HEAD).astype(jnp.bfloat16), pairs.reshape(2, TOKENS, KV_HEADS * HEAD).astype(jnp.bfloat16))


def tile_plan(key):
    devices = TILES // TILES_DEV
    permuted = jax.random.permutation(jax.random.fold_in(key, 101), TILES).astype(jnp.int32)
    window_start = jax.random.randint(jax.random.fold_in(key, 102), (devices, devices), 0, TILES_DEV)
    order_keys = jax.random.split(jax.random.fold_in(key, 103), devices)
    orders = jax.vmap(lambda one_key: jax.random.permutation(one_key, devices))(order_keys).astype(jnp.int32)
    home_dev = jnp.arange(TILES) // TILES_DEV
    local_index = jnp.arange(TILES) % TILES_DEV
    flat_entry = local_index[:, None] * ANC + jnp.arange(ANC)[None, :]
    source = orders[home_dev[:, None], flat_entry % devices]
    offset = window_start[home_dev[:, None], source]
    slot_ids = source * TILES_DEV + offset
    live_count = jax.random.randint(jax.random.fold_in(key, 105), (TILES,), max(2, ANC - 4), ANC + 1)
    heavy = home_dev % 4 == 0
    live_count = jnp.where(heavy, ANC, live_count)
    is_live = jnp.arange(ANC)[None, :] < live_count[:, None]
    tile_ids = jnp.where(is_live, permuted[slot_ids], -1)
    return (permuted, tile_ids.astype(jnp.int32))


def draw_query(key, part):
    return attention_inputs(key)[0]


def draw_keys_values(key, part):
    return attention_inputs(key)[1]


def draw_ancestors(key, part):
    return tile_plan(key)[1]


def draw_tile_of_slot(key, part):
    return tile_plan(key)[0]


def steps_of(key, dims, cuts, low, high):
    gain, own = 1.0, jax.random.fold_in(key, 6)
    for position, parts in cuts:
        heights = jnp.exp(jax.random.uniform(jax.random.fold_in(own, position), (parts,), jnp.float32, low / len(cuts), high / len(cuts)))
        gain = gain * jnp.repeat(heights, dims[position] // parts).reshape([-1 if axis == position else 1 for axis in range(len(dims))])
    return gain


def noise(stream_key, shape, width, limit, shards=(), kind=jnp.bfloat16):
    loudness = steps_of(stream_key, shape, shards, -0.22, 0.18) if shards else 1.0
    entries = jax.random.normal(stream_key, shape, jnp.float32) * width * loudness
    return jnp.minimum(jnp.maximum(entries, -limit), limit).astype(kind)


def setup_inputs(seed: int = 0) -> dict:
    arg_keys = jax.random.split(jax.random.key(seed), 8)
    return {
        "query": draw_query(jax.random.fold_in(arg_keys[7], 71), 0),
        "keys_values": draw_keys_values(jax.random.fold_in(arg_keys[7], 71), 0),
        "ancestors": draw_ancestors(jax.random.fold_in(arg_keys[7], 71), 0),
        "tile_of_slot": draw_tile_of_slot(jax.random.fold_in(arg_keys[7], 71), 0),
        "residual": noise(arg_keys[4], (TOKENS, D), 1.0, 6.0, ((0, 32), (1, 8))),
        "norm_gain": jnp.clip(1.0 + 0.15 * jax.random.normal(arg_keys[5], (D,), jnp.float32), 0.25, 1.75),
        "out_weight": noise(arg_keys[6], (HEADS * HEAD, D), (HEADS * HEAD) ** -0.5, 0.09375, ((0, 8),)),
    }


def slot_table(tile_of_slot, tile_count):
    numbers = jnp.arange(tile_count, dtype=jnp.int32)
    matches = tile_of_slot[None, :] == numbers[:, None]
    return lax.optimization_barrier(jnp.sum(jnp.where(matches, numbers[None, :], 0), axis=1)).astype(jnp.int32)

def live_slots(ancestors, slot_of, own_slots, tile_count):
    numbers = jnp.arange(tile_count, dtype=jnp.int32)
    matches = ancestors[:, :, None] == numbers[None, None, :]
    located = lax.optimization_barrier(jnp.sum(jnp.where(matches, slot_of[None, None, :], 0), axis=2)).astype(jnp.int32)
    located = jnp.where(ancestors >= 0, located, -1).astype(jnp.int32)
    width_anc = ancestors.shape[1]
    before = jnp.arange(width_anc)[:, None] > jnp.arange(width_anc)[None, :]
    repeated = jnp.any((located[:, :, None] == located[:, None, :]) & before[None], axis=2)
    keeping = (located >= 0) & (located != own_slots[:, None]) & jnp.logical_not(repeated)
    return jnp.where(keeping, located, -1).astype(jnp.int32)

def tile_attention(query_tile, key_own, value_own, key_far, value_far, far_live):
    kv_heads = key_own.shape[1]
    group_size = query_tile.shape[1] // (kv_heads * HEAD)
    score_scale = HEAD ** (-0.5)
    query_grid = query_tile.astype(jnp.float32).reshape(TILE, kv_heads, group_size, HEAD)
    near = jnp.einsum('qhgd,khd->hgqk', query_grid, key_own.astype(jnp.float32)) * score_scale
    causal = jnp.arange(TILE)[:, None] >= jnp.arange(TILE)[None, :]
    near = jnp.where(causal, near, -jnp.inf)
    far = jnp.einsum('qhgd,akhd->hgqak', query_grid, key_far.astype(jnp.float32)) * score_scale
    far = jnp.where(far_live[None, None, None, :, None], far, -jnp.inf)
    peak = jnp.maximum(lax.optimization_barrier(jnp.max(near, axis=3)), lax.optimization_barrier(jnp.max(far, axis=(3, 4))))
    near_weight = jnp.exp(near - peak[..., None])
    far_weight = jnp.exp(far - peak[..., None, None])
    totals = lax.optimization_barrier(jnp.sum(near_weight, axis=3)) + lax.optimization_barrier(jnp.sum(far_weight, axis=(3, 4)))
    near_round = lax.optimization_barrier(near_weight.astype(jnp.bfloat16)).astype(jnp.float32)
    far_round = lax.optimization_barrier(far_weight.astype(jnp.bfloat16)).astype(jnp.float32)
    mixed = jnp.einsum('hgqk,khd->hgqd', near_round, value_own.astype(jnp.float32))
    mixed = mixed + jnp.einsum('hgqak,akhd->hgqd', far_round, value_far.astype(jnp.float32))
    mixed = mixed / totals[..., None]
    return jnp.transpose(mixed, (2, 0, 1, 3)).reshape(TILE, kv_heads * group_size * HEAD).astype(jnp.bfloat16)

def reference(query, keys_values, ancestors, tile_of_slot, residual, norm_gain, out_weight):
    slot_of = slot_table(tile_of_slot, TILES)
    far_slots = live_slots(ancestors, slot_of, jnp.arange(TILES, dtype=jnp.int32), TILES)
    query_tiles = query.reshape(TILES, TILE, HEADS * HEAD)
    key_tiles = keys_values[0].reshape(TILES, TILE, KV_HEADS, HEAD)
    value_tiles = keys_values[1].reshape(TILES, TILE, KV_HEADS, HEAD)

    def one_tile(index):
        picked = jnp.clip(far_slots[index], 0, TILES - 1)
        return tile_attention(query_tiles[index], key_tiles[index], value_tiles[index], key_tiles[picked], value_tiles[picked], far_slots[index] >= 0)
    attended = lax.map(one_tile, jnp.arange(TILES, dtype=jnp.int32)).reshape(TOKENS, HEADS * HEAD)
    block_width = HEADS * HEAD // N_MP
    projected = jnp.zeros((TOKENS, D), jnp.float32)
    for block in range(N_MP):
        partial_term = jnp.dot(attended[:, block * block_width:(block + 1) * block_width], out_weight[block * block_width:(block + 1) * block_width], preferred_element_type=jnp.float32)
        partial_term = lax.optimization_barrier(partial_term.astype(jnp.bfloat16)).astype(jnp.float32)
        projected = projected + partial_term
    hidden_out = (residual.astype(jnp.float32) + projected).astype(jnp.bfloat16)
    hidden_f32 = hidden_out.astype(jnp.float32)
    mean_sq = lax.optimization_barrier(jnp.mean(hidden_f32 * hidden_f32, axis=1))
    normed = hidden_f32 * lax.rsqrt(mean_sq + 1e-05)[:, None] * norm_gain[None, :]
    return (hidden_out, normed.astype(jnp.bfloat16))
```

```python
import jax
import jax.numpy as jnp
from jax import lax
from jax.experimental import pallas as pl
from jax.experimental.pallas import tpu as pltpu
from jax.sharding import Mesh, PartitionSpec as P

D = 8192
HEAD = 128
TILE = 128
ANC = 12
NZ, NX, NY, NC = 8, 4, 4, 2
TILES = 64
BLOCK = 512
GROUP = 4
LOG2E = 1.4426950408889634
AXES = ("z", "x", "y", "c")


def permutation(target):
    pairs = []
    for z in range(NZ):
        for x in range(NX):
            for y in range(NY):
                for c in range(NC):
                    tz, tx, ty, tc = target(z, x, y, c)
                    source = ((z * NX + x) * NY + y) * NC + c
                    pairs.append(
                        (source, (((tz % NZ) * NX + tx % NX) * NY + ty % NY) * NC + tc % NC)
                    )
    return pairs


def along_z(array, hops):
    return lax.ppermute(
        array, AXES, permutation(lambda z, x, y, c: (z + hops * (1 - 2 * c), x, y, c))
    )


def along_x(array, hops):
    return lax.ppermute(array, AXES, permutation(lambda z, x, y, c: (z, x + hops, y, c)))


def along_y(array, hops):
    return lax.ppermute(array, AXES, permutation(lambda z, x, y, c: (z, x, y + hops, c)))


def other_core(array):
    return lax.ppermute(array, AXES, permutation(lambda z, x, y, c: (z, x, y, c + 1)))


def far_slots_of(ancestors, tile_of_slot, own_slots):
    numbers = jnp.arange(TILES, dtype=jnp.int32)
    matches = tile_of_slot[None, :] == numbers[:, None]
    slot_of = jnp.sum(jnp.where(matches, numbers[None, :], 0), axis=1)
    matches = ancestors[:, :, None] == numbers[None, None, :]
    located = jnp.sum(jnp.where(matches, slot_of[None, None, :], 0), axis=2)
    located = jnp.where(ancestors >= 0, located, -1)
    before = jnp.arange(ANC)[:, None] > jnp.arange(ANC)[None, :]
    repeated = jnp.any((located[:, :, None] == located[:, None, :]) & before[None], axis=2)
    keeping = (located >= 0) & (located != own_slots[:, None]) & jnp.logical_not(repeated)
    return jnp.where(keeping, located, -1)


def gather_pairs(own, z, x, c):
    sign = 1 - 2 * c

    def half(block):
        return lax.dynamic_slice_in_dim(block, c * 256, 256, 0)

    near1 = along_z(own, 1)
    near2 = along_z(own, 2)
    group2 = along_z(jnp.concatenate([own, half(near1)], axis=0), 3)
    group1 = jnp.concatenate([half(own), near1, near2], axis=0)
    up1, down1 = along_x(group1, 1), along_x(group1, -1)
    up2, down2 = along_x(group2, 1), along_x(group2, -1)
    upup1, downdown1 = along_x(up1[:640], 1), along_x(down1[640:], -1)
    upup2, downdown2 = along_x(up2[:384], 1), along_x(down2[384:], -1)

    def place(steps, hops, sgn):
        return (((z - steps * sgn) % NZ) * NX + (x + hops) % NX) * BLOCK

    def layout(sgn, part):
        def first(hops):
            return [
                (0, 256, place(0, hops, sgn) + 256 * part),
                (256, 512, place(1, hops, sgn)),
                (768, 512, place(2, hops, sgn)),
            ]

        def second(hops):
            return [
                (0, 512, place(3, hops, sgn)),
                (512, 256, place(4, hops, sgn) + 256 * part),
            ]

        return [
            [(0, 512, place(1, 0, sgn))],
            [(0, 512, place(2, 0, sgn))],
            second(0),
            first(-1),
            first(1),
            second(-1),
            second(1),
            [(0, 256, place(0, 2, sgn) + 256 * part), (256, 384, place(1, 2, sgn))],
            [(0, 128, place(1, 2, sgn) + 384), (128, 512, place(2, 2, sgn))],
            [(0, 384, place(3, 2, sgn))],
            [(0, 128, place(3, 2, sgn) + 384), (128, 256, place(4, 2, sgn) + 256 * part)],
        ]

    arrays = [near1, near2, group2, up1, down1, up2, down2, upup1, downdown1, upup2, downdown2]
    pieces = [(own, [(0, 512, place(0, 0, sign))])]
    pieces += list(zip(arrays, layout(sign, c)))
    pieces += list(zip([other_core(array) for array in arrays], layout(-sign, 1 - c)))
    return pieces


def attend(query, own, pieces, far_slots, base):
    spans = [[(row, rows) for row, rows, _ in spots] for _, spots in pieces]
    places = jnp.stack([spot[2] for _, spots in pieces for spot in spots]).astype(jnp.int32)
    arrays = [array for array, _ in pieces]
    far_bytes_scale = HEAD**-0.5 * LOG2E
    keys_total = (ANC + 1) * TILE

    def kernel(places_ref, far_ref, query_ref, own_ref, *rest):
        piece_refs = rest[: len(arrays)]
        out_ref, whole, keys, values, bias, sem = rest[len(arrays) :]
        copies = []
        for ref, ranges in zip(piece_refs, spans):
            for row, rows in ranges:
                start = pl.multiple_of(places_ref[len(copies)], 128)
                copies.append(
                    pltpu.make_async_copy(
                        ref.at[pl.ds(row, rows)], whole.at[pl.ds(start, rows)], sem
                    )
                )
        for copy in copies:
            copy.start()
        for copy in copies:
            copy.wait()
        rows_id = lax.broadcasted_iota(jnp.int32, (TILE, TILE), 0)
        cols_id = lax.broadcasted_iota(jnp.int32, (TILE, TILE), 1)
        causal = jnp.where(rows_id >= cols_id, 0.0, -jnp.inf)
        for t in range(2):
            keys[0:TILE] = own_ref[pl.ds(t * TILE, TILE)]
            values[0:TILE] = own_ref[pl.ds(256 + t * TILE, TILE)]
            for j in range(ANC):
                slot = far_ref[t, j]
                place = jnp.maximum(slot, 0)
                row = pl.multiple_of((place // 2) * BLOCK + (place % 2) * TILE, TILE)
                keys[(j + 1) * TILE : (j + 2) * TILE] = whole[pl.ds(row, TILE)]
                values[(j + 1) * TILE : (j + 2) * TILE] = whole[pl.ds(row + 256, TILE)]
                bias[:, (j + 1) * TILE : (j + 2) * TILE] = jnp.full(
                    (8, TILE), jnp.where(slot >= 0, 0.0, -jnp.inf), jnp.float32
                )
            for h in range(GROUP):
                q = query_ref[t * TILE : (t + 1) * TILE, h * HEAD : (h + 1) * HEAD]
                scores = lax.dot_general(
                    q, keys[...], (((1,), (1,)), ((), ())), preferred_element_type=jnp.float32
                )
                near = scores[:, :TILE] + causal
                far = scores[:, TILE:] + bias[0:1, TILE:]
                peak = jnp.maximum(
                    jnp.max(near, axis=1, keepdims=True), jnp.max(far, axis=1, keepdims=True)
                )
                near = jnp.exp2((near - peak) * far_bytes_scale)
                far = jnp.exp2((far - peak) * far_bytes_scale)
                total = jnp.sum(near, axis=1, keepdims=True) + jnp.sum(far, axis=1, keepdims=True)
                mixed = lax.dot_general(
                    near.astype(jnp.bfloat16),
                    values[0:TILE],
                    (((1,), (0,)), ((), ())),
                    preferred_element_type=jnp.float32,
                ) + lax.dot_general(
                    far.astype(jnp.bfloat16),
                    values[TILE:],
                    (((1,), (0,)), ((), ())),
                    preferred_element_type=jnp.float32,
                )
                out_ref[t * TILE : (t + 1) * TILE, h * HEAD : (h + 1) * HEAD] = (
                    mixed / total
                ).astype(jnp.bfloat16)

    return pl.pallas_call(
        kernel,
        out_shape=jax.ShapeDtypeStruct((2 * TILE, GROUP * HEAD), jnp.bfloat16),
        grid_spec=pltpu.PrefetchScalarGridSpec(
            num_scalar_prefetch=2,
            grid=(),
            in_specs=[
                pl.BlockSpec(memory_space=pltpu.VMEM),
                pl.BlockSpec(memory_space=pltpu.VMEM),
            ]
            + [pl.BlockSpec(memory_space=pl.ANY)] * len(arrays),
            out_specs=pl.BlockSpec(memory_space=pltpu.VMEM),
            scratch_shapes=[
                pltpu.VMEM((32 * BLOCK, HEAD), jnp.bfloat16),
                pltpu.VMEM((keys_total, HEAD), jnp.bfloat16),
                pltpu.VMEM((keys_total, HEAD), jnp.bfloat16),
                pltpu.VMEM((8, keys_total), jnp.float32),
                pltpu.SemaphoreType.DMA,
            ],
        ),
        name="attend",
    )(places, far_slots, query, own, *arrays)


def project(attended, attended_other, weight, weight_other, blocks):
    tile_n = 512
    per = 1024 // tile_n
    count = len(blocks)

    def kernel(blocks_ref, a_ref, b_ref, w_ref, v_ref, out_ref):
        term = jnp.dot(a_ref[...], w_ref[...], preferred_element_type=jnp.float32)
        term += jnp.dot(b_ref[...], v_ref[...], preferred_element_type=jnp.float32)
        out_ref[0] = term.astype(jnp.bfloat16)

    def w_map(k, i, blocks_ref):
        return (0, blocks_ref[k] * per + i)

    return pl.pallas_call(
        kernel,
        out_shape=jax.ShapeDtypeStruct((count, 256, 1024), jnp.bfloat16),
        grid_spec=pltpu.PrefetchScalarGridSpec(
            num_scalar_prefetch=1,
            grid=(count, per),
            in_specs=[
                pl.BlockSpec((256, 512), lambda k, i, r: (0, 0)),
                pl.BlockSpec((256, 512), lambda k, i, r: (0, 0)),
                pl.BlockSpec((512, tile_n), w_map),
                pl.BlockSpec((512, tile_n), w_map),
            ],
            out_specs=pl.BlockSpec((1, 256, tile_n), lambda k, i, r: (k, 0, i)),
        ),
        name="project",
    )(jnp.stack(blocks).astype(jnp.int32), attended, attended_other, weight, weight_other)


def body(query, keys_values, ancestors, tile_of_slot, residual, norm_gain, out_weight):
    z, x, y, c = (lax.axis_index(name) for name in AXES)
    weight_other = other_core(out_weight)
    own = lax.dynamic_slice_in_dim(keys_values, y * HEAD, HEAD, 2).reshape(BLOCK, HEAD)
    own_slots = (z * NX + x) * 2 + jnp.arange(2, dtype=jnp.int32)
    far_slots = far_slots_of(ancestors, tile_of_slot, own_slots)
    pieces = gather_pairs(own, z, x, c)
    attended = attend(query, own, pieces, far_slots, None)
    attended_other = other_core(attended)

    def block(hops):
        return ((y + hops) % NY) * 2 + c

    args = (attended, attended_other, out_weight, weight_other)
    across = project(*args, [block(2)])[0]
    relay_up = along_y(across[:TILE], 1)
    relay_down = along_y(across[TILE:], -1)
    sides = project(*args, [block(1), block(3)])
    low_up = along_y(sides[0, TILE:], 1)
    high_down = along_y(sides[1, :TILE], -1)
    high_up = along_y(sides[0, :TILE] + relay_up, 1)
    low_down = along_y(sides[1, TILE:] + relay_down, -1)
    here = project(*args, [block(0)])[0].astype(jnp.float32)
    high = high_up.astype(jnp.float32) + high_down.astype(jnp.float32)
    low = low_up.astype(jnp.float32) + low_down.astype(jnp.float32)
    total = here + jnp.concatenate([high, low], axis=0)
    hidden_out = (residual.astype(jnp.float32) + total).astype(jnp.bfloat16)
    hidden_f32 = hidden_out.astype(jnp.float32)
    squares = jnp.sum(hidden_f32 * hidden_f32, axis=1)
    copies = jnp.broadcast_to(squares[None, None], (NY * NC, 1, squares.shape[0]))
    mean_sq = jnp.sum(lax.all_to_all(copies, ("y", "c"), 0, 0, tiled=True), axis=(0, 1)) / D
    normed = hidden_f32 * lax.rsqrt(mean_sq + 1e-05)[:, None] * norm_gain[None, :]
    return (hidden_out, normed.astype(jnp.bfloat16))


def solution(mesh):
    fine = Mesh(mesh.devices.reshape(NZ, NX, NY, NC), AXES)
    rows, columns = ("z", "x"), ("y", "c")
    return jax.shard_map(
        body,
        mesh=fine,
        in_specs=(
            P(rows, columns),
            P(None, rows, None),
            P(rows, None),
            P(),
            P(rows, columns),
            P(columns),
            P(columns, None),
        ),
        out_specs=(P(rows, columns), P(rows, columns)),
        check_vma=False,
    )
```

```python
import jax
import jax.numpy as jnp
from jax import lax
from jax.experimental import pallas as pl
from jax.experimental.pallas import tpu as pltpu
from jax.sharding import Mesh, PartitionSpec as P


D = 8192
HEAD = 128
TILE = 128
ANC = 12
NZ, NX, NY, NC = 8, 4, 4, 2
TILES = 64
BLOCK = 512
GROUP = 4
LOG2E = 1.4426950408889634
AXES = ("z", "x", "y", "c")


def permutation(target):
    pairs = []
    for z in range(NZ):
        for x in range(NX):
            for y in range(NY):
                for c in range(NC):
                    tz, tx, ty, tc = target(z, x, y, c)
                    source = ((z * NX + x) * NY + y) * NC + c
                    pairs.append(
                        (source, (((tz % NZ) * NX + tx % NX) * NY + ty % NY) * NC + tc % NC)
                    )
    return pairs


def along_z(array, hops):
    return lax.ppermute(
        array, AXES, permutation(lambda z, x, y, c: (z + hops * (1 - 2 * c), x, y, c))
    )


def along_x(array, hops):
    return lax.ppermute(
        array, AXES, permutation(lambda z, x, y, c: (z, x + hops * (1 - 2 * c), y, c))
    )


def along_y(array, hops):
    return lax.ppermute(
        array, AXES, permutation(lambda z, x, y, c: (z, x, y + hops * (1 - 2 * c), c))
    )


def other_core(array):
    return lax.ppermute(array, AXES, permutation(lambda z, x, y, c: (z, x, y, c + 1)))


def gather_pairs(own, c):
    def half(block):
        return lax.dynamic_slice_in_dim(block, c * 256, 256, 0)

    near1 = along_z(own, 1)
    near2 = along_z(own, 2)
    near3 = along_z(own, 3)
    half4 = along_z(half(own), 4)
    group1 = jnp.concatenate([half(own), near1, near2], axis=0)
    ahead1 = along_x(group1, 1)
    back1 = along_x(group1, -1)
    group2 = jnp.concatenate([near3, half4], axis=0)
    ahead2 = along_x(group2, 1)
    back2 = along_x(group2, -1)
    far1, far1_low = along_x(ahead1[:640], 1), along_x(back1[640:], -1)
    far2, far2_low = along_x(ahead2[:384], 1), along_x(back2[384:], -1)
    arrays = [near1, near2, group2, ahead1, back1, ahead2, back2, far1, far1_low, far2, far2_low]
    return arrays, [other_core(array) for array in arrays]


def spot(refs, steps, hops, row):
    near1, near2, group2, ahead1, back1, ahead2, back2, far1, far1_low, far2, far2_low = refs
    if hops == 0 and steps < 3:
        return (near1, near2)[steps - 1], row
    row += {0: 0, 1: 256, 2: 768, 3: 0, 4: 512}[steps]
    if steps < 3:
        held, far, cut = (None, ahead1, None, back1)[hops], (far1, far1_low), 640
    else:
        held, far, cut = (group2, ahead2, None, back2)[hops], (far2, far2_low), 384
    if hops == 2:
        return (far[0], row) if row < cut else (far[1], row - cut)
    return held, row


def attend(query, own, mine, theirs, ancestors, tile_of_slot):
    scale = HEAD**-0.5 * LOG2E
    keys_total = (ANC + 1) * TILE
    count = len(mine)

    def kernel(ancestors_hbm, tile_of_slot_hbm, query_hbm, own_ref, *rest):
        mine_refs, theirs_refs = rest[:count], rest[count : 2 * count]
        out_ref, keys, values, scores, weights, bias, query_ref = rest[2 * count : 2 * count + 7]
        ancestors_ref, tile_of_slot_ref, slot_of, wanted, sems = rest[2 * count + 7 :]
        z, x, c = (lax.axis_index(name) for name in ("z", "x", "c"))
        sign = 1 - 2 * c
        copies = [
            pltpu.make_async_copy(ancestors_hbm, ancestors_ref, sems.at[0]),
            pltpu.make_async_copy(tile_of_slot_hbm, tile_of_slot_ref, sems.at[1]),
            pltpu.make_async_copy(query_hbm, query_ref, sems.at[2]),
        ]
        for copy in copies:
            copy.start()
        for copy in copies[:2]:
            copy.wait()
        for s in range(TILES):
            slot_of[tile_of_slot_ref[s]] = s
        for t in range(2):
            start = t * keys_total
            keys[start : start + TILE] = own_ref[t * TILE : (t + 1) * TILE]
            values[start : start + TILE] = own_ref[256 + t * TILE : 256 + (t + 1) * TILE]
            own_slot = (z * NX + x) * 2 + t
            located = []
            for j in range(ANC):
                tile = ancestors_ref[t, j]
                slot = jnp.where(tile >= 0, slot_of[jnp.maximum(tile, 0)], -1)
                keep = jnp.logical_and(slot >= 0, slot != own_slot)
                for earlier in located:
                    keep = jnp.logical_and(keep, slot != earlier)
                located.append(slot)
                wanted[t * ANC + j] = jnp.where(keep, slot, own_slot)
                bias[t, :, (j + 1) * TILE : (j + 2) * TILE] = jnp.full(
                    (8, TILE), jnp.where(keep, 0.0, -jnp.inf), jnp.float32
                )

        def take(i, carry):
            slot = wanted[i]
            second = slot % 2
            chip = slot // 2
            steps = lax.rem((z - chip // NX) * sign + NZ, NZ)
            hops = lax.rem((x - chip % NX) * sign + NX, NX)
            to = pl.multiple_of((i + 1 + jnp.where(i >= ANC, 1, 0)) * TILE, TILE)

            def put(target, source, row):
                start = pl.multiple_of(row + second * TILE, TILE)
                target[pl.ds(to, TILE)] = source[pl.ds(start, TILE)]

            def put_from(target, refs, n, h, row):
                (ref0, row0), (ref1, row1) = (spot(refs, n, h, row + r) for r in (0, TILE))
                if ref0 is ref1:
                    put(target, ref0, row0)
                else:

                    @pl.when(second == 0)
                    def _():
                        target[pl.ds(to, TILE)] = ref0[row0 : row0 + TILE]

                    @pl.when(second == 1)
                    def _():
                        target[pl.ds(to, TILE)] = ref1[row1 : row1 + TILE]

            def from_chip(n, h):
                h_other = (NX - h) % NX
                if n == 0 and h == 0:
                    put(keys, own_ref, 0)
                    put(values, own_ref, 256)
                elif n in (0, 4):

                    @pl.when(c == 0)
                    def _():
                        put_from(keys, mine_refs, n, h, 0)
                        put_from(values, theirs_refs, n, h_other, 0)

                    @pl.when(c == 1)
                    def _():
                        put_from(keys, theirs_refs, n, h_other, 0)
                        put_from(values, mine_refs, n, h, 0)

                elif n < 4:
                    put_from(keys, mine_refs, n, h, 0)
                    put_from(values, mine_refs, n, h, 256)
                else:
                    put_from(keys, theirs_refs, NZ - n, h_other, 0)
                    put_from(values, theirs_refs, NZ - n, h_other, 256)

            for h in range(NX):

                @pl.when(hops == h)
                def _(h=h):
                    for n in range(NZ):

                        @pl.when(steps == n)
                        def _(n=n):
                            from_chip(n, h)

            return carry

        lax.fori_loop(0, 2 * ANC, take, 0)
        copies[2].wait()
        rows_id = lax.broadcasted_iota(jnp.int32, (TILE, TILE), 0)
        cols_id = lax.broadcasted_iota(jnp.int32, (TILE, TILE), 1)
        causal = jnp.where(rows_id >= cols_id, 0.0, -jnp.inf)
        for t in range(2):
            q = jnp.concatenate(
                [
                    query_ref[t * TILE : (t + 1) * TILE, h * HEAD : (h + 1) * HEAD]
                    for h in range(GROUP)
                ],
                axis=0,
            )
            scores[t] = lax.dot_general(
                q,
                keys[t * keys_total : (t + 1) * keys_total],
                (((1,), (1,)), ((), ())),
                preferred_element_type=jnp.float32,
            )
        for t in range(2):
            totals = []
            for h in range(GROUP):
                rows = slice(h * TILE, (h + 1) * TILE)
                near = scores[t, rows, :TILE] + causal
                far = scores[t, rows, TILE:] + bias[t, 0:1, TILE:]
                peak = jnp.maximum(
                    jnp.max(near, axis=1, keepdims=True), jnp.max(far, axis=1, keepdims=True)
                )
                near = jnp.exp2((near - peak) * scale)
                far = jnp.exp2((far - peak) * scale)
                totals.append(
                    jnp.sum(near, axis=1, keepdims=True) + jnp.sum(far, axis=1, keepdims=True)
                )
                weights[t, rows, :TILE] = near.astype(jnp.bfloat16)
                weights[t, rows, TILE:] = far.astype(jnp.bfloat16)
            mixed = jnp.dot(
                weights[t],
                values[t * keys_total : (t + 1) * keys_total],
                preferred_element_type=jnp.float32,
            )
            for h in range(GROUP):
                out_ref[t * TILE : (t + 1) * TILE, h * HEAD : (h + 1) * HEAD] = (
                    mixed[h * TILE : (h + 1) * TILE] / totals[h]
                ).astype(jnp.bfloat16)

    return pl.pallas_call(
        kernel,
        out_shape=jax.ShapeDtypeStruct((2 * TILE, GROUP * HEAD), jnp.bfloat16),
        in_specs=[pl.BlockSpec(memory_space=pltpu.HBM)] * 3
        + [pl.BlockSpec(memory_space=pltpu.VMEM)] * (1 + 2 * count),
        out_specs=pl.BlockSpec(memory_space=pltpu.VMEM),
        scratch_shapes=[
            pltpu.VMEM((2 * keys_total, HEAD), jnp.bfloat16),
            pltpu.VMEM((2 * keys_total, HEAD), jnp.bfloat16),
            pltpu.VMEM((2, GROUP * TILE, keys_total), jnp.float32),
            pltpu.VMEM((2, GROUP * TILE, keys_total), jnp.bfloat16),
            pltpu.VMEM((2, 8, keys_total), jnp.float32),
            pltpu.VMEM((2 * TILE, GROUP * HEAD), jnp.bfloat16),
            pltpu.SMEM((2, ANC), jnp.int32),
            pltpu.SMEM((TILES,), jnp.int32),
            pltpu.SMEM((TILES,), jnp.int32),
            pltpu.SMEM((2 * ANC,), jnp.int32),
            pltpu.SemaphoreType.DMA((3,)),
        ],
        compiler_params=pltpu.CompilerParams(vmem_limit_bytes=28 << 20),
        name="attend",
    )(
        *(pltpu.with_memory_space_constraint(a, pltpu.HBM) for a in (ancestors, tile_of_slot, query)),
        own,
        *mine,
        *theirs,
    )


def fetch(weight, weight_other):
    def kernel(weight_ref, other_ref, out_ref, sem):
        y, c = lax.axis_index("y"), lax.axis_index("c")
        sign = 1 - 2 * c
        copies = []
        for hops in range(NY):
            column = pl.multiple_of((lax.rem(y + hops * sign + NY, NY) * 2 + c) * 1024, 1024)
            for ref, row in ((weight_ref, 0), (other_ref, 512)):
                copies.append(
                    pltpu.make_async_copy(
                        ref.at[:, pl.ds(column, 1024)], out_ref.at[hops, pl.ds(row, 512)], sem
                    )
                )
        for copy in copies:
            copy.start()
        for copy in copies:
            copy.wait()

    return pl.pallas_call(
        kernel,
        out_shape=pltpu.VMEM((NY, 1024, 1024), jnp.bfloat16),
        in_specs=[pl.BlockSpec(memory_space=pltpu.HBM)] * 2,
        out_specs=pl.BlockSpec(memory_space=pltpu.VMEM),
        scratch_shapes=[pltpu.SemaphoreType.DMA],
        compiler_params=pltpu.CompilerParams(vmem_limit_bytes=12 << 20),
        name="fetch",
    )(
        pltpu.with_memory_space_constraint(weight, pltpu.HBM),
        pltpu.with_memory_space_constraint(weight_other, pltpu.HBM),
    )


def project(attended, attended_other, weights, parts, added=(), dtype=jnp.bfloat16):
    count = len(parts)
    sizes = [2 * TILE if tile is None else TILE for _, tile in parts]

    def kernel(a_ref, b_ref, w_ref, *rest):
        added_refs, out_refs = rest[: len(added)], rest[len(added) :]
        c = lax.axis_index("c")
        for k, ((hops, tile), rows) in enumerate(zip(parts, sizes)):
            row = 0 if tile is None else pl.multiple_of((c if tile == 0 else 1 - c) * TILE, TILE)
            for n in range(0, 1024, 256):
                term = jnp.dot(
                    a_ref[pl.ds(row, rows)],
                    w_ref[hops, 0:512, n : n + 256],
                    preferred_element_type=jnp.float32,
                )
                term += jnp.dot(
                    b_ref[pl.ds(row, rows)],
                    w_ref[hops, 512:1024, n : n + 256],
                    preferred_element_type=jnp.float32,
                )
                if added:
                    term += added_refs[k][:, n : n + 256].astype(jnp.float32)
                out_refs[k][:, n : n + 256] = term.astype(dtype)

    return pl.pallas_call(
        kernel,
        out_shape=[jax.ShapeDtypeStruct((rows, 1024), dtype) for rows in sizes],
        in_specs=[pl.BlockSpec(memory_space=pltpu.VMEM)] * (3 + len(added)),
        out_specs=[pl.BlockSpec(memory_space=pltpu.VMEM)] * count,
        compiler_params=pltpu.CompilerParams(vmem_limit_bytes=16 << 20),
        name="project",
    )(attended, attended_other, weights, *added)


def layer(query, keys_values, ancestors, tile_of_slot, residual, norm_gain, out_weight):
    y, c = lax.axis_index("y"), lax.axis_index("c")
    own = lax.dynamic_slice_in_dim(keys_values, y * HEAD, HEAD, 2).reshape(BLOCK, HEAD)
    weight_other = other_core(out_weight)
    weights = fetch(out_weight, weight_other)
    mine, theirs = gather_pairs(own, c)
    attended = attend(query, own, mine, theirs, ancestors, tile_of_slot)
    args = (attended, other_core(attended), weights)
    across0, across1 = project(*args, [(2, 0), (2, 1)])
    relay_ahead = along_y(across0, 1)
    relay_back = along_y(across1, -1)
    direct1, direct0 = project(*args, [(1, 1), (3, 0)])
    from_back1 = along_y(direct1, 1)
    from_ahead0 = along_y(direct0, -1)
    joined0, joined1 = project(*args, [(1, 0), (3, 1)], (relay_ahead, relay_back))
    from_back0 = along_y(joined0, 1)
    from_ahead1 = along_y(joined1, -1)
    (here,) = project(*args, [(0, None)], (), jnp.float32)
    share0 = from_back0.astype(jnp.float32) + from_ahead0.astype(jnp.float32)
    share1 = from_ahead1.astype(jnp.float32) + from_back1.astype(jnp.float32)
    total = here + jnp.where(
        c == 0,
        jnp.concatenate([share0, share1], axis=0),
        jnp.concatenate([share1, share0], axis=0),
    )
    hidden_out = (residual.astype(jnp.float32) + total).astype(jnp.bfloat16)
    hidden_f32 = hidden_out.astype(jnp.float32)
    squares = jnp.sum(hidden_f32 * hidden_f32, axis=1)
    copies = jnp.broadcast_to(squares[None, None], (NY * NC, 1, squares.shape[0]))
    mean_sq = jnp.sum(lax.all_to_all(copies, ("y", "c"), 0, 0, tiled=True), axis=(0, 1)) / D
    normed = hidden_f32 * lax.rsqrt(mean_sq + 1e-05)[:, None] * norm_gain[None, :]
    return (hidden_out, normed.astype(jnp.bfloat16))


def solution(mesh):
    fine = Mesh(mesh.devices.reshape(NZ, NX, NY, NC), AXES)
    rows, columns = ("z", "x"), ("y", "c")
    return jax.shard_map(
        layer,
        mesh=fine,
        in_specs=(
            P(rows, columns),
            P(None, rows, None),
            P(rows, None),
            P(),
            P(rows, columns),
            P(columns),
            P(columns, None),
        ),
        out_specs=(P(rows, columns), P(rows, columns)),
        check_vma=False,
    )
```

```python
import jax
import jax.numpy as jnp
from jax import lax
from jax.experimental import pallas as pl
from jax.experimental.pallas import tpu as pltpu
from jax.sharding import Mesh, PartitionSpec as P


D = 8192
HEAD = 128
TILE = 128
ANC = 12
NZ, NX, NY, NC = 8, 4, 4, 2
TILES = 64
BLOCK = 512
GROUP = 4
LOG2E = 1.4426950408889634
AXES = ("z", "x", "y", "c")


def permutation(target):
    pairs = []
    for z in range(NZ):
        for x in range(NX):
            for y in range(NY):
                for c in range(NC):
                    tz, tx, ty, tc = target(z, x, y, c)
                    source = ((z * NX + x) * NY + y) * NC + c
                    pairs.append(
                        (source, (((tz % NZ) * NX + tx % NX) * NY + ty % NY) * NC + tc % NC)
                    )
    return pairs


def along_z(array, hops):
    return lax.ppermute(
        array, AXES, permutation(lambda z, x, y, c: (z + hops * (1 - 2 * c), x, y, c))
    )


def along_x(array, hops):
    return lax.ppermute(
        array, AXES, permutation(lambda z, x, y, c: (z, x + hops * (1 - 2 * c), y, c))
    )


def along_y(array, hops):
    return lax.ppermute(
        array, AXES, permutation(lambda z, x, y, c: (z, x, y + hops * (1 - 2 * c), c))
    )


def other_core(array):
    return lax.ppermute(array, AXES, permutation(lambda z, x, y, c: (z, x, y, c + 1)))


def gather_pairs(own, own_half):
    near1 = along_z(own, 1)
    near2 = along_z(own, 2)
    near3 = along_z(near1, 2)
    half4 = along_z(lax.dynamic_slice_in_dim(near2, lax.axis_index("c") * 256, 256, 0), 2)
    group1 = jnp.concatenate([own_half, near1, near2], axis=0)
    ahead1 = along_x(group1, 1)
    back1 = along_x(group1, -1)
    group2 = jnp.concatenate([near3, half4], axis=0)
    ahead2 = along_x(group2, 1)
    back2 = along_x(group2, -1)
    far1 = along_x(ahead1[:640], 1)
    far1_low = along_x(back1[640:], -1)
    far2 = along_x(ahead2[:384], 1)
    far2_low = along_x(back2[384:], -1)
    arrays = [near1, near2, group2, ahead1, back1, ahead2, back2, far1, far1_low, far2, far2_low]
    theirs = []
    for array in arrays:
        theirs.append(other_core(array))
    return arrays, theirs


def pick(keys_values):
    def kernel(all_ref, block_ref, half_ref, sems):
        y, c = lax.axis_index("y"), lax.axis_index("c")
        head = all_ref.at[:, :, pl.ds(pl.multiple_of(y * HEAD, HEAD), HEAD)]
        copies = [
            pltpu.make_async_copy(head, block_ref, sems.at[0]),
            pltpu.make_async_copy(head.at[c], half_ref, sems.at[1]),
        ]
        for copy in copies:
            copy.start()
        for copy in copies:
            copy.wait()

    return pl.pallas_call(
        kernel,
        out_shape=[
            pltpu.VMEM((2, 256, HEAD), jnp.bfloat16),
            pltpu.VMEM((256, HEAD), jnp.bfloat16),
        ],
        in_specs=[pl.BlockSpec(memory_space=pltpu.HBM)],
        out_specs=[pl.BlockSpec(memory_space=pltpu.VMEM)] * 2,
        scratch_shapes=[pltpu.SemaphoreType.DMA((2,))],
        name="pick",
    )(pltpu.with_memory_space_constraint(keys_values, pltpu.HBM))


def spot(refs, steps, hops, row):
    near1, near2, group2, ahead1, back1, ahead2, back2, far1, far1_low, far2, far2_low = refs
    if hops == 0 and steps < 3:
        return (near1, near2)[steps - 1], row
    row += {0: 0, 1: 256, 2: 768, 3: 0, 4: 512}[steps]
    if steps < 3:
        held, far, cut = (None, ahead1, None, back1)[hops], (far1, far1_low), 640
    else:
        held, far, cut = (group2, ahead2, None, back2)[hops], (far2, far2_low), 384
    if hops == 2:
        return (far[0], row) if row < cut else (far[1], row - cut)
    return held, row


def attend(query, own, mine, theirs, ancestors, tile_of_slot, weight, weight_other):
    scale = HEAD**-0.5 * LOG2E
    keys_total = (ANC + 1) * TILE
    count = len(mine)

    def kernel(ancestors_hbm, tile_of_slot_hbm, query_hbm, *rest):
        weight_refs, own_ref, rest = rest[:2], rest[2], rest[3:]
        mine_refs, theirs_refs = rest[:count], rest[count : 2 * count]
        out_ref, *loaded_refs = rest[2 * count : 2 * count + 3]
        keys, values, scores, weights, bias, query_ref = rest[2 * count + 3 : 2 * count + 9]
        ancestors_ref, tile_of_slot_ref, slot_of, wanted, sems = rest[2 * count + 9 :]
        z, x, y, c = (lax.axis_index(name) for name in AXES)
        sign = 1 - 2 * c
        copies = [
            pltpu.make_async_copy(ancestors_hbm, ancestors_ref, sems.at[0]),
            pltpu.make_async_copy(tile_of_slot_hbm, tile_of_slot_ref, sems.at[1]),
            pltpu.make_async_copy(query_hbm, query_ref, sems.at[2]),
        ]
        for copy in copies:
            copy.start()
        loads = []
        for hops in (2, 1, 3, 0):
            column = pl.multiple_of((lax.rem(y + hops * sign + NY, NY) * 2 + c) * 1024, 1024)
            for source, target in zip(weight_refs, loaded_refs):
                loads.append(
                    pltpu.make_async_copy(
                        source.at[:, pl.ds(column, 1024)], target.at[hops], sems.at[3]
                    )
                )
        for copy in loads:
            copy.start()
        for copy in copies[:2]:
            copy.wait()
        for s in range(TILES):
            slot_of[tile_of_slot_ref[s]] = s
        for t in range(2):
            start = t * keys_total
            keys[start : start + TILE] = own_ref[t * TILE : (t + 1) * TILE]
            values[start : start + TILE] = own_ref[256 + t * TILE : 256 + (t + 1) * TILE]
            own_slot = (z * NX + x) * 2 + t
            located = []
            for j in range(ANC):
                tile = ancestors_ref[t, j]
                slot = jnp.where(tile >= 0, slot_of[jnp.maximum(tile, 0)], -1)
                keep = jnp.logical_and(slot >= 0, slot != own_slot)
                for earlier in located:
                    keep = jnp.logical_and(keep, slot != earlier)
                located.append(slot)
                wanted[t * ANC + j] = jnp.where(keep, slot, own_slot)
                bias[t, :, (j + 1) * TILE : (j + 2) * TILE] = jnp.full(
                    (8, TILE), jnp.where(keep, 0.0, -jnp.inf), jnp.float32
                )

        def take(i, carry):
            slot = wanted[i]
            second = slot % 2
            chip = slot // 2
            steps = lax.rem((z - chip // NX) * sign + NZ, NZ)
            hops = lax.rem((x - chip % NX) * sign + NX, NX)
            to = pl.multiple_of((i + 1 + jnp.where(i >= ANC, 1, 0)) * TILE, TILE)

            def put(target, source, row):
                start = pl.multiple_of(row + second * TILE, TILE)
                target[pl.ds(to, TILE)] = source[pl.ds(start, TILE)]

            def put_from(target, refs, n, h, row):
                (ref0, row0), (ref1, row1) = (spot(refs, n, h, row + r) for r in (0, TILE))
                if ref0 is ref1:
                    put(target, ref0, row0)
                else:

                    @pl.when(second == 0)
                    def _():
                        target[pl.ds(to, TILE)] = ref0[row0 : row0 + TILE]

                    @pl.when(second == 1)
                    def _():
                        target[pl.ds(to, TILE)] = ref1[row1 : row1 + TILE]

            def from_chip(n, h):
                h_other = (NX - h) % NX
                if n == 0 and h == 0:
                    put(keys, own_ref, 0)
                    put(values, own_ref, 256)
                elif n in (0, 4):

                    @pl.when(c == 0)
                    def _():
                        put_from(keys, mine_refs, n, h, 0)
                        put_from(values, theirs_refs, n, h_other, 0)

                    @pl.when(c == 1)
                    def _():
                        put_from(keys, theirs_refs, n, h_other, 0)
                        put_from(values, mine_refs, n, h, 0)

                elif n < 4:
                    put_from(keys, mine_refs, n, h, 0)
                    put_from(values, mine_refs, n, h, 256)
                else:
                    put_from(keys, theirs_refs, NZ - n, h_other, 0)
                    put_from(values, theirs_refs, NZ - n, h_other, 256)

            def branch(case, low, high):
                if high - low == 1:
                    from_chip(low % NZ, low // NZ)
                    return
                middle = (low + high) // 2
                lax.cond(
                    case < middle,
                    lambda: branch(case, low, middle),
                    lambda: branch(case, middle, high),
                )

            branch(hops * NZ + steps, 0, NX * NZ)
            return carry

        lax.fori_loop(0, 2 * ANC, take, 0)
        copies[2].wait()
        rows_id = lax.broadcasted_iota(jnp.int32, (TILE, TILE), 0)
        cols_id = lax.broadcasted_iota(jnp.int32, (TILE, TILE), 1)
        causal = jnp.where(rows_id >= cols_id, 0.0, -jnp.inf)
        for t in range(2):
            q = jnp.concatenate(
                [
                    query_ref[t * TILE : (t + 1) * TILE, h * HEAD : (h + 1) * HEAD]
                    for h in range(GROUP)
                ],
                axis=0,
            )
            scores[t] = lax.dot_general(
                q,
                keys[t * keys_total : (t + 1) * keys_total],
                (((1,), (1,)), ((), ())),
                preferred_element_type=jnp.float32,
            )
        for t in range(2):
            totals = []
            for h in range(GROUP):
                rows = slice(h * TILE, (h + 1) * TILE)
                near = scores[t, rows, :TILE] + causal
                far = scores[t, rows, TILE:] + bias[t, 0:1, TILE:]
                peak = jnp.maximum(
                    jnp.max(near, axis=1, keepdims=True), jnp.max(far, axis=1, keepdims=True)
                )
                near = jnp.exp2((near - peak) * scale)
                far = jnp.exp2((far - peak) * scale)
                totals.append(
                    jnp.sum(near, axis=1, keepdims=True) + jnp.sum(far, axis=1, keepdims=True)
                )
                weights[t, rows, :TILE] = near.astype(jnp.bfloat16)
                weights[t, rows, TILE:] = far.astype(jnp.bfloat16)
            mixed = jnp.dot(
                weights[t],
                values[t * keys_total : (t + 1) * keys_total],
                preferred_element_type=jnp.float32,
            )
            for h in range(GROUP):
                out_ref[t * TILE : (t + 1) * TILE, h * HEAD : (h + 1) * HEAD] = (
                    mixed[h * TILE : (h + 1) * TILE] / totals[h]
                ).astype(jnp.bfloat16)
        for copy in loads:
            copy.wait()

    return pl.pallas_call(
        kernel,
        out_shape=[
            pltpu.VMEM((2 * TILE, GROUP * HEAD), jnp.bfloat16),
            pltpu.VMEM((NY, 512, 1024), jnp.bfloat16),
            pltpu.VMEM((NY, 512, 1024), jnp.bfloat16),
        ],
        in_specs=[pl.BlockSpec(memory_space=pltpu.HBM)] * 5
        + [pl.BlockSpec(memory_space=pltpu.VMEM)] * (1 + 2 * count),
        out_specs=[pl.BlockSpec(memory_space=pltpu.VMEM)] * 3,
        scratch_shapes=[
            pltpu.VMEM((2 * keys_total, HEAD), jnp.bfloat16),
            pltpu.VMEM((2 * keys_total, HEAD), jnp.bfloat16),
            pltpu.VMEM((2, GROUP * TILE, keys_total), jnp.float32),
            pltpu.VMEM((2, GROUP * TILE, keys_total), jnp.bfloat16),
            pltpu.VMEM((2, 8, keys_total), jnp.float32),
            pltpu.VMEM((2 * TILE, GROUP * HEAD), jnp.bfloat16),
            pltpu.SMEM((2, ANC), jnp.int32),
            pltpu.SMEM((TILES,), jnp.int32),
            pltpu.SMEM((TILES,), jnp.int32),
            pltpu.SMEM((2 * ANC,), jnp.int32),
            pltpu.SemaphoreType.DMA((4,)),
        ],
        compiler_params=pltpu.CompilerParams(vmem_limit_bytes=28 << 20),
        name="attend",
    )(
        *(
            pltpu.with_memory_space_constraint(array, pltpu.HBM)
            for array in (ancestors, tile_of_slot, query, weight, weight_other)
        ),
        own,
        *mine,
        *theirs,
    )


def project(attended, attended_other, weights, weights_other, parts, added=(), dtype=jnp.bfloat16):
    count = len(parts)
    sizes = [2 * TILE if tile is None else TILE for _, tile in parts]

    def kernel(a_ref, b_ref, w_ref, v_ref, *rest):
        added_refs, out_refs = rest[: len(added)], rest[len(added) :]
        c = lax.axis_index("c")
        for k, ((hops, tile), rows) in enumerate(zip(parts, sizes)):
            row = 0 if tile is None else pl.multiple_of((c if tile == 0 else 1 - c) * TILE, TILE)
            for n in range(0, 1024, 256):
                term = jnp.dot(
                    a_ref[pl.ds(row, rows)],
                    w_ref[hops, :, n : n + 256],
                    preferred_element_type=jnp.float32,
                )
                term += jnp.dot(
                    b_ref[pl.ds(row, rows)],
                    v_ref[hops, :, n : n + 256],
                    preferred_element_type=jnp.float32,
                )
                if added:
                    term += added_refs[k][:, n : n + 256].astype(jnp.float32)
                out_refs[k][:, n : n + 256] = term.astype(dtype)

    return pl.pallas_call(
        kernel,
        out_shape=[jax.ShapeDtypeStruct((rows, 1024), dtype) for rows in sizes],
        in_specs=[pl.BlockSpec(memory_space=pltpu.VMEM)] * (4 + len(added)),
        out_specs=[pl.BlockSpec(memory_space=pltpu.VMEM)] * count,
        compiler_params=pltpu.CompilerParams(vmem_limit_bytes=16 << 20),
        name="project",
    )(attended, attended_other, weights, weights_other, *added)


def finish(here, from_back0, from_ahead0, from_ahead1, from_back1, residual):
    def kernel(here_ref, b0_ref, a0_ref, a1_ref, b1_ref, residual_ref, hidden_ref, sums_ref):
        c = lax.axis_index("c")
        ones = jnp.ones((8, 128), jnp.float32)
        for tile, first_ref, second_ref in ((c, b0_ref, a0_ref), (1 - c, a1_ref, b1_ref)):
            row = pl.multiple_of(tile * TILE, TILE)
            squares = jnp.zeros((TILE, 128), jnp.float32)
            for n in range(0, 1024, 128):
                columns = slice(n, n + 128)
                share = first_ref[:, columns].astype(jnp.float32)
                share += second_ref[:, columns].astype(jnp.float32)
                share += here_ref[pl.ds(row, TILE), columns]
                share += residual_ref[pl.ds(row, TILE), columns].astype(jnp.float32)
                hidden = share.astype(jnp.bfloat16)
                hidden_ref[pl.ds(row, TILE), columns] = hidden
                hidden = hidden.astype(jnp.float32)
                squares += hidden * hidden
            sums = lax.dot_general(
                ones,
                squares,
                (((1,), (1,)), ((), ())),
                precision=lax.Precision.HIGHEST,
                preferred_element_type=jnp.float32,
            )
            for k in range(NY * NC):
                sums_ref[k, :, pl.ds(row, TILE)] = sums[0:1]

    return pl.pallas_call(
        kernel,
        out_shape=[
            pltpu.VMEM((2 * TILE, 1024), jnp.bfloat16),
            pltpu.VMEM((NY * NC, 1, 2 * TILE), jnp.float32),
        ],
        in_specs=[pl.BlockSpec(memory_space=pltpu.VMEM)] * 6,
        out_specs=[pl.BlockSpec(memory_space=pltpu.VMEM)] * 2,
        compiler_params=pltpu.CompilerParams(vmem_limit_bytes=8 << 20),
        name="finish",
    )(here, from_back0, from_ahead0, from_ahead1, from_back1, residual)


def normalize(hidden, sums, gain):
    def kernel(hidden_ref, sums_ref, gain_ref, hidden_hbm, normed_hbm, normed_ref, sems):
        out = pltpu.make_async_copy(hidden_ref, hidden_hbm, sems.at[0])
        out.start()
        copies = []
        for tile in range(2):
            rows = slice(tile * TILE, (tile + 1) * TILE)
            total = sums_ref[0, :, rows]
            for k in range(1, NY * NC):
                total += sums_ref[k, :, rows]
            scale = lax.rsqrt(jnp.broadcast_to(total, (TILE, TILE)) / D + 1e-05)
            scale = jnp.transpose(scale)
            for n in range(0, 1024, 128):
                columns = slice(n, n + 128)
                normed_ref[rows, columns] = (
                    hidden_ref[rows, columns].astype(jnp.float32) * scale * gain_ref[:, columns]
                ).astype(jnp.bfloat16)
            copies.append(
                pltpu.make_async_copy(normed_ref.at[rows], normed_hbm.at[rows], sems.at[1 + tile])
            )
            copies[-1].start()
        out.wait()
        for copy in copies:
            copy.wait()

    shape = jax.ShapeDtypeStruct((2 * TILE, 1024), jnp.bfloat16)
    return pl.pallas_call(
        kernel,
        out_shape=[shape, shape],
        in_specs=[pl.BlockSpec(memory_space=pltpu.VMEM)] * 3,
        out_specs=[pl.BlockSpec(memory_space=pltpu.HBM)] * 2,
        scratch_shapes=[
            pltpu.VMEM((2 * TILE, 1024), jnp.bfloat16),
            pltpu.SemaphoreType.DMA((3,)),
        ],
        compiler_params=pltpu.CompilerParams(vmem_limit_bytes=8 << 20),
        name="normalize",
    )(hidden, sums, gain.reshape(1, 1024))


def layer(query, keys_values, ancestors, tile_of_slot, residual, norm_gain, out_weight):
    own, own_half = pick(keys_values)
    own = own.reshape(BLOCK, HEAD)
    weight_other = other_core(out_weight)
    mine, theirs = gather_pairs(own, own_half)
    attended, *weights = attend(
        query, own, mine, theirs, ancestors, tile_of_slot, out_weight, weight_other
    )
    args = (attended, other_core(attended), *weights)
    across0, across1 = project(*args, [(2, 0), (2, 1)])
    relay_ahead = along_y(across0, 1)
    relay_back = along_y(across1, -1)
    direct1, direct0 = project(*args, [(1, 1), (3, 0)])
    from_back1 = along_y(direct1, 1)
    from_ahead0 = along_y(direct0, -1)
    joined0, joined1 = project(*args, [(1, 0), (3, 1)], (relay_ahead, relay_back))
    from_back0 = along_y(joined0, 1)
    from_ahead1 = along_y(joined1, -1)
    (here,) = project(*args, [(0, None)], (), jnp.float32)
    hidden, sums = finish(here, from_back0, from_ahead0, from_ahead1, from_back1, residual)
    sums = lax.all_to_all(sums, ("y", "c"), 0, 0, tiled=True)
    return tuple(normalize(hidden, sums, norm_gain))


def solution(mesh):
    fine = Mesh(mesh.devices.reshape(NZ, NX, NY, NC), AXES)
    rows, columns = ("z", "x"), ("y", "c")
    return jax.shard_map(
        layer,
        mesh=fine,
        in_specs=(
            P(rows, columns),
            P(None, rows, None),
            P(rows, None),
            P(),
            P(rows, columns),
            P(columns),
            P(columns, None),
        ),
        out_specs=(P(rows, columns), P(rows, columns)),
        check_vma=False,
    )
```

```python
import jax
import jax.numpy as jnp
from jax import lax
from jax.experimental import pallas as pl
from jax.experimental.pallas import tpu as pltpu
from jax.sharding import Mesh, PartitionSpec as P


D = 8192
HEAD = 128
TILE = 128
ANC = 12
NZ, NX, NY, NC = 8, 4, 4, 2
TILES = 64
BLOCK = 512
GROUP = 4
LOG2E = 1.4426950408889634
AXES = ("z", "x", "y", "c")


def permutation(target):
    pairs = []
    for z in range(NZ):
        for x in range(NX):
            for y in range(NY):
                for c in range(NC):
                    tz, tx, ty, tc = target(z, x, y, c)
                    source = ((z * NX + x) * NY + y) * NC + c
                    pairs.append(
                        (source, (((tz % NZ) * NX + tx % NX) * NY + ty % NY) * NC + tc % NC)
                    )
    return pairs


def along_z(array, hops):
    return lax.ppermute(
        array, AXES, permutation(lambda z, x, y, c: (z + hops * (1 - 2 * c), x, y, c))
    )


def along_x(array, hops):
    return lax.ppermute(
        array, AXES, permutation(lambda z, x, y, c: (z, x + hops * (1 - 2 * c), y, c))
    )


def along_y(array, hops):
    return lax.ppermute(
        array, AXES, permutation(lambda z, x, y, c: (z, x, y + hops * (1 - 2 * c), c))
    )


def other_core(array):
    return lax.ppermute(array, AXES, permutation(lambda z, x, y, c: (z, x, y, c + 1)))


def choose(ancestors, tile_of_slot):
    def kernel(first_ref, second_ref, third_ref, tile_of_slot_ref, out_ref):
        z, x, c = (lax.axis_index(name) for name in ("z", "x", "c"))
        sign = 1 - 2 * c
        slots = lax.broadcasted_iota(jnp.int32, (1, TILES), 1)
        for n in range(NZ):
            slot = (lax.rem(z - n * sign + NZ, NZ) * NX + x) * 2 + 1
            tile = jnp.sum(
                jnp.where(slots == slot, tile_of_slot_ref[...], 0), axis=1, keepdims=True
            )
            for k, ref in enumerate((first_ref, second_ref, third_ref)):
                named = jnp.where(ref[...] == tile, 1.0, 0.0)
                named = jnp.max(jnp.max(named, axis=1, keepdims=True), axis=0, keepdims=True)
                out_ref[k * NZ + n : k * NZ + n + 1, :] = jnp.broadcast_to(named, (1, 128))

    return pl.pallas_call(
        kernel,
        out_shape=pltpu.VMEM((3 * NZ, 128), jnp.float32),
        in_specs=[pl.BlockSpec(memory_space=pltpu.VMEM)] * 4,
        out_specs=pl.BlockSpec(memory_space=pltpu.VMEM),
        compiler_params=pltpu.CompilerParams(vmem_limit_bytes=4 << 20),
        name="choose",
    )(*ancestors, tile_of_slot.reshape(1, TILES))


def select(chosen, arrays, steps):
    total = sum(array.shape[0] for array in arrays) // 2

    def kernel(chosen_ref, *refs):
        array_refs, out_refs = refs[: len(arrays)], refs[len(arrays) :]
        for k, out_ref in enumerate(out_refs):
            to = 0
            for ref, n in zip(array_refs, steps):
                second = chosen_ref[k * NZ + n : k * NZ + n + 1, :]
                first = jnp.broadcast_to(1.0 - second, (TILE, 128)).astype(jnp.bfloat16)
                second = jnp.broadcast_to(second, (TILE, 128)).astype(jnp.bfloat16)
                for row in range(0, ref.shape[0], 2 * TILE):
                    out_ref[to : to + TILE] = (
                        ref[row : row + TILE] * first + ref[row + TILE : row + 2 * TILE] * second
                    )
                    to += TILE

    return pl.pallas_call(
        kernel,
        out_shape=[pltpu.VMEM((total, HEAD), jnp.bfloat16)] * 3,
        in_specs=[pl.BlockSpec(memory_space=pltpu.VMEM)] * (1 + len(arrays)),
        out_specs=[pl.BlockSpec(memory_space=pltpu.VMEM)] * 3,
        compiler_params=pltpu.CompilerParams(vmem_limit_bytes=4 << 20),
        name="select",
    )(chosen, *arrays)


def gather_pairs(own, own_half, ancestors, tile_of_slot):
    asked_ahead = along_x(ancestors, -1)
    asked_back = along_x(ancestors, 1)
    asked_across = along_x(ancestors, 2)
    near1 = along_z(own, 1)
    near2 = along_z(own, 2)
    near3 = along_z(near1, 2)
    half4 = along_z(lax.dynamic_slice_in_dim(near2, lax.axis_index("c") * 256, 256, 0), 2)
    chosen = choose((asked_ahead, asked_back, asked_across), tile_of_slot)
    arrays = [near1, near2, near3, half4]
    for parts, steps in (((own_half, near1, near2), (0, 1, 2)), ((near3, half4), (3, 4))):
        messages = select(chosen, parts, steps)
        for hops, message in reversed(tuple(zip((1, -1, 2), messages))):
            arrays.append(along_x(message, hops))
    theirs = []
    for array in arrays:
        theirs.append(other_core(array))
    return arrays, theirs


def pick(keys_values):
    def kernel(all_ref, block_ref, half_ref, sems):
        y, c = lax.axis_index("y"), lax.axis_index("c")
        head = all_ref.at[:, :, pl.ds(pl.multiple_of(y * HEAD, HEAD), HEAD)]
        copies = [
            pltpu.make_async_copy(head, block_ref, sems.at[0]),
            pltpu.make_async_copy(head.at[c], half_ref, sems.at[1]),
        ]
        for copy in copies:
            copy.start()
        for copy in copies:
            copy.wait()

    return pl.pallas_call(
        kernel,
        out_shape=[
            pltpu.VMEM((2, 256, HEAD), jnp.bfloat16),
            pltpu.VMEM((256, HEAD), jnp.bfloat16),
        ],
        in_specs=[pl.BlockSpec(memory_space=pltpu.HBM)],
        out_specs=[pl.BlockSpec(memory_space=pltpu.VMEM)] * 2,
        scratch_shapes=[pltpu.SemaphoreType.DMA((2,))],
        compiler_params=pltpu.CompilerParams(vmem_limit_bytes=4 << 20),
        name="pick",
    )(pltpu.with_memory_space_constraint(keys_values, pltpu.HBM))


def spot(refs, steps, hops, part):
    whole, (across1, back1, ahead1, across2, back2, ahead2) = refs[:4], refs[4:]
    if hops == 0:
        return whole[steps - 1], (0 if steps == 4 else 256 * part), True
    row = {0: 0, 1: 128, 2: 384, 3: 0, 4: 256}[steps] + (0 if steps in (0, 4) else 128 * part)
    first, second = {1: (ahead1, ahead2), 3: (back1, back2), 2: (across1, across2)}[hops]
    return (first if steps < 3 else second), row, False


def attend(query, own, mine, theirs, ancestors, tile_of_slot, weight, weight_other):
    scale = HEAD**-0.5 * LOG2E
    keys_total = (ANC + 1) * TILE
    count = len(mine)

    def kernel(ancestors_hbm, tile_of_slot_hbm, query_hbm, *rest):
        weight_refs, own_ref, rest = rest[:2], rest[2], rest[3:]
        mine_refs, theirs_refs = rest[:count], rest[count : 2 * count]
        out_ref, *loaded_refs = rest[2 * count : 2 * count + 3]
        keys, values, scores, weights, bias, query_ref = rest[2 * count + 3 : 2 * count + 9]
        ancestors_ref, tile_of_slot_ref, slot_of, wanted, sems = rest[2 * count + 9 :]
        z, x, y, c = (lax.axis_index(name) for name in AXES)
        sign = 1 - 2 * c
        copies = [
            pltpu.make_async_copy(ancestors_hbm, ancestors_ref, sems.at[0]),
            pltpu.make_async_copy(tile_of_slot_hbm, tile_of_slot_ref, sems.at[1]),
            pltpu.make_async_copy(query_hbm, query_ref, sems.at[2]),
        ]
        for copy in copies:
            copy.start()
        loads = []
        for hops in (2, 1, 3, 0):
            column = pl.multiple_of((lax.rem(y + hops * sign + NY, NY) * 2 + c) * 1024, 1024)
            for source, target in zip(weight_refs, loaded_refs):
                loads.append(
                    pltpu.make_async_copy(
                        source.at[:, pl.ds(column, 1024)], target.at[hops], sems.at[3]
                    )
                )
        for copy in loads:
            copy.start()
        for copy in copies[:2]:
            copy.wait()
        for s in range(TILES):
            slot_of[tile_of_slot_ref[s]] = s
        for t in range(2):
            start = t * keys_total
            keys[start : start + TILE] = own_ref[t * TILE : (t + 1) * TILE]
            values[start : start + TILE] = own_ref[256 + t * TILE : 256 + (t + 1) * TILE]
            own_slot = (z * NX + x) * 2 + t
            located = []
            for j in range(ANC):
                tile = ancestors_ref[t, j]
                slot = jnp.where(tile >= 0, slot_of[jnp.maximum(tile, 0)], -1)
                keep = jnp.logical_and(slot >= 0, slot != own_slot)
                for earlier in located:
                    keep = jnp.logical_and(keep, slot != earlier)
                located.append(slot)
                wanted[t * ANC + j] = jnp.where(keep, slot, own_slot)
                bias[t, :, (j + 1) * TILE : (j + 2) * TILE] = jnp.full(
                    (8, TILE), jnp.where(keep, 0.0, -jnp.inf), jnp.float32
                )

        def take(i, carry):
            slot = wanted[i]
            second = slot % 2
            chip = slot // 2
            steps = lax.rem((z - chip // NX) * sign + NZ, NZ)
            hops = lax.rem((x - chip % NX) * sign + NX, NX)
            to = pl.multiple_of((i + 1 + jnp.where(i >= ANC, 1, 0)) * TILE, TILE)

            def put(target, source, row, both):
                start = pl.multiple_of(row + second * TILE, TILE) if both else row
                target[pl.ds(to, TILE)] = source[pl.ds(start, TILE)]

            def from_chip(n, h):
                h_other = (NX - h) % NX
                if n == 0 and h == 0:
                    put(keys, own_ref, 0, True)
                    put(values, own_ref, 256, True)
                elif n in (0, 4):

                    @pl.when(c == 0)
                    def _():
                        put(keys, *spot(mine_refs, n, h, 0))
                        put(values, *spot(theirs_refs, n, h_other, 1))

                    @pl.when(c == 1)
                    def _():
                        put(keys, *spot(theirs_refs, n, h_other, 0))
                        put(values, *spot(mine_refs, n, h, 1))

                elif n < 4:
                    put(keys, *spot(mine_refs, n, h, 0))
                    put(values, *spot(mine_refs, n, h, 1))
                else:
                    put(keys, *spot(theirs_refs, NZ - n, h_other, 0))
                    put(values, *spot(theirs_refs, NZ - n, h_other, 1))

            def branch(case, low, high):
                if high - low == 1:
                    from_chip(low % NZ, low // NZ)
                    return
                middle = (low + high) // 2
                lax.cond(
                    case < middle,
                    lambda: branch(case, low, middle),
                    lambda: branch(case, middle, high),
                )

            branch(hops * NZ + steps, 0, NX * NZ)
            return carry

        lax.fori_loop(0, 2 * ANC, take, 0)
        copies[2].wait()
        rows_id = lax.broadcasted_iota(jnp.int32, (TILE, TILE), 0)
        cols_id = lax.broadcasted_iota(jnp.int32, (TILE, TILE), 1)
        causal = jnp.where(rows_id >= cols_id, 0.0, -jnp.inf)
        for t in range(2):
            q = jnp.concatenate(
                [
                    query_ref[t * TILE : (t + 1) * TILE, h * HEAD : (h + 1) * HEAD]
                    for h in range(GROUP)
                ],
                axis=0,
            )
            scores[t] = lax.dot_general(
                q,
                keys[t * keys_total : (t + 1) * keys_total],
                (((1,), (1,)), ((), ())),
                preferred_element_type=jnp.float32,
            )
        for t in range(2):
            totals = []
            for h in range(GROUP):
                rows = slice(h * TILE, (h + 1) * TILE)
                near = scores[t, rows, :TILE] + causal
                far = scores[t, rows, TILE:] + bias[t, 0:1, TILE:]
                peak = jnp.maximum(
                    jnp.max(near, axis=1, keepdims=True), jnp.max(far, axis=1, keepdims=True)
                )
                near = jnp.exp2((near - peak) * scale)
                far = jnp.exp2((far - peak) * scale)
                totals.append(
                    jnp.sum(near, axis=1, keepdims=True) + jnp.sum(far, axis=1, keepdims=True)
                )
                weights[t, rows, :TILE] = near.astype(jnp.bfloat16)
                weights[t, rows, TILE:] = far.astype(jnp.bfloat16)
            mixed = jnp.dot(
                weights[t],
                values[t * keys_total : (t + 1) * keys_total],
                preferred_element_type=jnp.float32,
            )
            for h in range(GROUP):
                out_ref[t * TILE : (t + 1) * TILE, h * HEAD : (h + 1) * HEAD] = (
                    mixed[h * TILE : (h + 1) * TILE] / totals[h]
                ).astype(jnp.bfloat16)
        for copy in loads:
            copy.wait()

    return pl.pallas_call(
        kernel,
        out_shape=[
            pltpu.VMEM((2 * TILE, GROUP * HEAD), jnp.bfloat16),
            pltpu.VMEM((NY, 512, 1024), jnp.bfloat16),
            pltpu.VMEM((NY, 512, 1024), jnp.bfloat16),
        ],
        in_specs=[pl.BlockSpec(memory_space=pltpu.HBM)] * 5
        + [pl.BlockSpec(memory_space=pltpu.VMEM)] * (1 + 2 * count),
        out_specs=[pl.BlockSpec(memory_space=pltpu.VMEM)] * 3,
        scratch_shapes=[
            pltpu.VMEM((2 * keys_total, HEAD), jnp.bfloat16),
            pltpu.VMEM((2 * keys_total, HEAD), jnp.bfloat16),
            pltpu.VMEM((2, GROUP * TILE, keys_total), jnp.float32),
            pltpu.VMEM((2, GROUP * TILE, keys_total), jnp.bfloat16),
            pltpu.VMEM((2, 8, keys_total), jnp.float32),
            pltpu.VMEM((2 * TILE, GROUP * HEAD), jnp.bfloat16),
            pltpu.SMEM((2, ANC), jnp.int32),
            pltpu.SMEM((TILES,), jnp.int32),
            pltpu.SMEM((TILES,), jnp.int32),
            pltpu.SMEM((2 * ANC,), jnp.int32),
            pltpu.SemaphoreType.DMA((4,)),
        ],
        compiler_params=pltpu.CompilerParams(vmem_limit_bytes=28 << 20),
        name="attend",
    )(
        *(
            pltpu.with_memory_space_constraint(array, pltpu.HBM)
            for array in (ancestors, tile_of_slot, query, weight, weight_other)
        ),
        own,
        *mine,
        *theirs,
    )


def project(attended, attended_other, weights, weights_other, parts, added=(), dtype=jnp.bfloat16):
    count = len(parts)
    sizes = [2 * TILE if tile is None else TILE for _, tile in parts]

    def kernel(a_ref, b_ref, w_ref, v_ref, *rest):
        added_refs, out_refs = rest[: len(added)], rest[len(added) :]
        c = lax.axis_index("c")
        for k, ((hops, tile), rows) in enumerate(zip(parts, sizes)):
            row = 0 if tile is None else pl.multiple_of((c if tile == 0 else 1 - c) * TILE, TILE)
            for n in range(0, 1024, 256):
                term = jnp.dot(
                    a_ref[pl.ds(row, rows)],
                    w_ref[hops, :, n : n + 256],
                    preferred_element_type=jnp.float32,
                )
                term += jnp.dot(
                    b_ref[pl.ds(row, rows)],
                    v_ref[hops, :, n : n + 256],
                    preferred_element_type=jnp.float32,
                )
                if added:
                    term += added_refs[k][:, n : n + 256].astype(jnp.float32)
                out_refs[k][:, n : n + 256] = term.astype(dtype)

    return pl.pallas_call(
        kernel,
        out_shape=[jax.ShapeDtypeStruct((rows, 1024), dtype) for rows in sizes],
        in_specs=[pl.BlockSpec(memory_space=pltpu.VMEM)] * (4 + len(added)),
        out_specs=[pl.BlockSpec(memory_space=pltpu.VMEM)] * count,
        compiler_params=pltpu.CompilerParams(vmem_limit_bytes=16 << 20),
        name="project",
    )(attended, attended_other, weights, weights_other, *added)


def finish(here, from_back0, from_ahead0, from_ahead1, from_back1, residual):
    def kernel(here_ref, b0_ref, a0_ref, a1_ref, b1_ref, residual_ref, hidden_ref, sums_ref):
        c = lax.axis_index("c")
        ones = jnp.ones((8, 128), jnp.float32)
        for tile, first_ref, second_ref in ((c, b0_ref, a0_ref), (1 - c, a1_ref, b1_ref)):
            row = pl.multiple_of(tile * TILE, TILE)
            squares = jnp.zeros((TILE, 128), jnp.float32)
            for n in range(0, 1024, 128):
                columns = slice(n, n + 128)
                share = first_ref[:, columns].astype(jnp.float32)
                share += second_ref[:, columns].astype(jnp.float32)
                share += here_ref[pl.ds(row, TILE), columns]
                share += residual_ref[pl.ds(row, TILE), columns].astype(jnp.float32)
                hidden = share.astype(jnp.bfloat16)
                hidden_ref[pl.ds(row, TILE), columns] = hidden
                hidden = hidden.astype(jnp.float32)
                squares += hidden * hidden
            sums = lax.dot_general(
                ones,
                squares,
                (((1,), (1,)), ((), ())),
                precision=lax.Precision.HIGHEST,
                preferred_element_type=jnp.float32,
            )
            for k in range(NY * NC):
                sums_ref[k, :, pl.ds(row, TILE)] = sums[0:1]

    return pl.pallas_call(
        kernel,
        out_shape=[
            pltpu.VMEM((2 * TILE, 1024), jnp.bfloat16),
            pltpu.VMEM((NY * NC, 1, 2 * TILE), jnp.float32),
        ],
        in_specs=[pl.BlockSpec(memory_space=pltpu.VMEM)] * 6,
        out_specs=[pl.BlockSpec(memory_space=pltpu.VMEM)] * 2,
        compiler_params=pltpu.CompilerParams(vmem_limit_bytes=8 << 20),
        name="finish",
    )(here, from_back0, from_ahead0, from_ahead1, from_back1, residual)


def normalize(hidden, sums, gain):
    def kernel(hidden_ref, sums_ref, gain_ref, hidden_hbm, normed_hbm, normed_ref, sems):
        out = pltpu.make_async_copy(hidden_ref, hidden_hbm, sems.at[0])
        out.start()
        copies = []
        for tile in range(2):
            rows = slice(tile * TILE, (tile + 1) * TILE)
            total = sums_ref[0, :, rows]
            for k in range(1, NY * NC):
                total += sums_ref[k, :, rows]
            scale = lax.rsqrt(jnp.broadcast_to(total, (TILE, TILE)) / D + 1e-05)
            scale = jnp.transpose(scale)
            for n in range(0, 1024, 128):
                columns = slice(n, n + 128)
                normed_ref[rows, columns] = (
                    hidden_ref[rows, columns].astype(jnp.float32) * scale * gain_ref[:, columns]
                ).astype(jnp.bfloat16)
            copies.append(
                pltpu.make_async_copy(normed_ref.at[rows], normed_hbm.at[rows], sems.at[1 + tile])
            )
            copies[-1].start()
        out.wait()
        for copy in copies:
            copy.wait()

    shape = jax.ShapeDtypeStruct((2 * TILE, 1024), jnp.bfloat16)
    return pl.pallas_call(
        kernel,
        out_shape=[shape, shape],
        in_specs=[pl.BlockSpec(memory_space=pltpu.VMEM)] * 3,
        out_specs=[pl.BlockSpec(memory_space=pltpu.HBM)] * 2,
        scratch_shapes=[
            pltpu.VMEM((2 * TILE, 1024), jnp.bfloat16),
            pltpu.SemaphoreType.DMA((3,)),
        ],
        compiler_params=pltpu.CompilerParams(vmem_limit_bytes=8 << 20),
        name="normalize",
    )(hidden, sums, gain.reshape(1, 1024))


def layer(query, keys_values, ancestors, tile_of_slot, residual, norm_gain, out_weight):
    own, own_half = pick(keys_values)
    own = own.reshape(BLOCK, HEAD)
    weight_other = other_core(out_weight)
    mine, theirs = gather_pairs(own, own_half, ancestors, tile_of_slot)
    attended, *weights = attend(
        query, own, mine, theirs, ancestors, tile_of_slot, out_weight, weight_other
    )
    args = (attended, other_core(attended), *weights)
    across0, across1 = project(*args, [(2, 0), (2, 1)])
    relay_ahead = along_y(across0, 1)
    relay_back = along_y(across1, -1)
    direct1, direct0 = project(*args, [(1, 1), (3, 0)])
    from_back1 = along_y(direct1, 1)
    from_ahead0 = along_y(direct0, -1)
    joined0, joined1 = project(*args, [(1, 0), (3, 1)], (relay_ahead, relay_back))
    from_back0 = along_y(joined0, 1)
    from_ahead1 = along_y(joined1, -1)
    (here,) = project(*args, [(0, None)], (), jnp.float32)
    hidden, sums = finish(here, from_back0, from_ahead0, from_ahead1, from_back1, residual)
    sums = lax.all_to_all(sums, ("y", "c"), 0, 0, tiled=True)
    return tuple(normalize(hidden, sums, norm_gain))


def solution(mesh):
    fine = Mesh(mesh.devices.reshape(NZ, NX, NY, NC), AXES)
    rows, columns = ("z", "x"), ("y", "c")
    return jax.shard_map(
        layer,
        mesh=fine,
        in_specs=(
            P(rows, columns),
            P(None, rows, None),
            P(rows, None),
            P(),
            P(rows, columns),
            P(columns),
            P(columns, None),
        ),
        out_specs=(P(rows, columns), P(rows, columns)),
        check_vma=False,
    )
```

```python
import jax
import jax.numpy as jnp
from jax import lax
from jax.experimental import pallas as pl
from jax.experimental.pallas import tpu as pltpu
from jax.sharding import Mesh, PartitionSpec as P


D = 8192
HEAD = 128
TILE = 128
ANC = 12
NZ, NX, NY, NC = 8, 4, 4, 2
TILES = 64
BLOCK = 512
GROUP = 4
LOG2E = 1.4426950408889634
AXES = ("z", "x", "y", "c")


def permutation(target):
    pairs = []
    for z in range(NZ):
        for x in range(NX):
            for y in range(NY):
                for c in range(NC):
                    tz, tx, ty, tc = target(z, x, y, c)
                    source = ((z * NX + x) * NY + y) * NC + c
                    pairs.append(
                        (source, (((tz % NZ) * NX + tx % NX) * NY + ty % NY) * NC + tc % NC)
                    )
    return pairs


def along_z(array, hops):
    return lax.ppermute(
        array, AXES, permutation(lambda z, x, y, c: (z + hops * (1 - 2 * c), x, y, c))
    )


def along_x(array, hops):
    return lax.ppermute(
        array, AXES, permutation(lambda z, x, y, c: (z, x + hops * (1 - 2 * c), y, c))
    )


def along_y(array, hops):
    return lax.ppermute(
        array, AXES, permutation(lambda z, x, y, c: (z, x, y + hops * (1 - 2 * c), c))
    )


def other_core(array):
    return lax.ppermute(array, AXES, permutation(lambda z, x, y, c: (z, x, y, c + 1)))


def choose(ancestors, tile_of_slot):
    def kernel(first_ref, second_ref, third_ref, tile_of_slot_ref, out_ref):
        z, x, c = (lax.axis_index(name) for name in ("z", "x", "c"))
        sign = 1 - 2 * c
        slots = lax.broadcasted_iota(jnp.int32, (1, TILES), 1)
        for n in range(NZ):
            slot = (lax.rem(z - n * sign + NZ, NZ) * NX + x) * 2 + 1
            tile = jnp.sum(
                jnp.where(slots == slot, tile_of_slot_ref[...], 0), axis=1, keepdims=True
            )
            for k, ref in enumerate((first_ref, second_ref, third_ref)):
                named = jnp.where(ref[...] == tile, 1.0, 0.0)
                named = jnp.max(jnp.max(named, axis=1, keepdims=True), axis=0, keepdims=True)
                out_ref[k * NZ + n : k * NZ + n + 1, :] = jnp.broadcast_to(named, (1, 128))

    return pl.pallas_call(
        kernel,
        out_shape=pltpu.VMEM((3 * NZ, 128), jnp.float32),
        in_specs=[pl.BlockSpec(memory_space=pltpu.VMEM)] * 4,
        out_specs=pl.BlockSpec(memory_space=pltpu.VMEM),
        compiler_params=pltpu.CompilerParams(vmem_limit_bytes=4 << 20),
        name="choose",
    )(*ancestors, tile_of_slot)


def select(chosen, arrays, steps):
    total = sum(array.shape[0] for array in arrays) // 2

    def kernel(chosen_ref, *refs):
        array_refs, out_refs = refs[: len(arrays)], refs[len(arrays) :]
        for k, out_ref in enumerate(out_refs):
            to = 0
            for ref, n in zip(array_refs, steps):
                second = chosen_ref[k * NZ + n : k * NZ + n + 1, :]
                first = jnp.broadcast_to(1.0 - second, (TILE, 128)).astype(jnp.bfloat16)
                second = jnp.broadcast_to(second, (TILE, 128)).astype(jnp.bfloat16)
                for row in range(0, ref.shape[0], 2 * TILE):
                    out_ref[to : to + TILE] = (
                        ref[row : row + TILE] * first + ref[row + TILE : row + 2 * TILE] * second
                    )
                    to += TILE

    return pl.pallas_call(
        kernel,
        out_shape=[pltpu.VMEM((total, HEAD), jnp.bfloat16)] * 3,
        in_specs=[pl.BlockSpec(memory_space=pltpu.VMEM)] * (1 + len(arrays)),
        out_specs=[pl.BlockSpec(memory_space=pltpu.VMEM)] * 3,
        compiler_params=pltpu.CompilerParams(vmem_limit_bytes=4 << 20),
        name="select",
    )(chosen, *arrays)


def gather_pairs(own, own_half, ancestors, tile_of_slot):
    asked_ahead = along_x(ancestors, -1)
    asked_back = along_x(ancestors, 1)
    asked_across = along_x(ancestors, 2)
    near1 = along_z(own, 1)
    near2 = along_z(own, 2)
    near3 = along_z(near1, 2)
    half4 = along_z(lax.dynamic_slice_in_dim(near2, lax.axis_index("c") * 256, 256, 0), 2)
    chosen = choose((asked_ahead, asked_back, asked_across), tile_of_slot)
    arrays = [near1, near2, near3, half4]
    for parts, steps in (((own_half, near1, near2), (0, 1, 2)), ((near3, half4), (3, 4))):
        messages = select(chosen, parts, steps)
        for hops, message in reversed(tuple(zip((1, -1, 2), messages))):
            arrays.append(along_x(message, hops))
    theirs = []
    for array in arrays:
        theirs.append(other_core(array))
    return arrays, theirs


def pick(keys_values, ancestors, tile_of_slot):
    def kernel(all_ref, anc_hbm, tiles_hbm, block_ref, half_ref, anc_ref, tiles_ref, sems):
        y, c = lax.axis_index("y"), lax.axis_index("c")
        head = all_ref.at[:, :, pl.ds(pl.multiple_of(y * HEAD, HEAD), HEAD)]
        copies = [
            pltpu.make_async_copy(head, block_ref, sems.at[0]),
            pltpu.make_async_copy(head.at[c], half_ref, sems.at[1]),
            pltpu.make_async_copy(anc_hbm, anc_ref, sems.at[2]),
            pltpu.make_async_copy(tiles_hbm, tiles_ref, sems.at[3]),
        ]
        for copy in copies:
            copy.start()
        for copy in copies:
            copy.wait()

    return pl.pallas_call(
        kernel,
        out_shape=[
            pltpu.VMEM((2, 256, HEAD), jnp.bfloat16),
            pltpu.VMEM((256, HEAD), jnp.bfloat16),
            pltpu.VMEM((2, ANC), jnp.int32),
            pltpu.VMEM((1, TILES), jnp.int32),
        ],
        in_specs=[pl.BlockSpec(memory_space=pltpu.HBM)] * 3,
        out_specs=[pl.BlockSpec(memory_space=pltpu.VMEM)] * 4,
        scratch_shapes=[pltpu.SemaphoreType.DMA((4,))],
        compiler_params=pltpu.CompilerParams(vmem_limit_bytes=4 << 20),
        name="pick",
    )(
        *(
            pltpu.with_memory_space_constraint(array, pltpu.HBM)
            for array in (keys_values, ancestors, tile_of_slot.reshape(1, TILES))
        )
    )


def spot(refs, steps, hops, part):
    whole, (across1, back1, ahead1, across2, back2, ahead2) = refs[:4], refs[4:]
    if hops == 0:
        return whole[steps - 1], (0 if steps == 4 else 256 * part), True
    row = {0: 0, 1: 128, 2: 384, 3: 0, 4: 256}[steps] + (0 if steps in (0, 4) else 128 * part)
    first, second = {1: (ahead1, ahead2), 3: (back1, back2), 2: (across1, across2)}[hops]
    return (first if steps < 3 else second), row, False


def attend(query, own, mine, theirs, ancestors, tile_of_slot, weight, weight_other):
    scale = HEAD**-0.5 * LOG2E
    keys_total = (ANC + 1) * TILE
    count = len(mine)

    def kernel(query_hbm, *rest):
        weight_refs, rest = rest[:2], rest[2:]
        (ancestors_vmem, tile_of_slot_vmem, own_ref), rest = rest[:3], rest[3:]
        mine_refs, theirs_refs = rest[:count], rest[count : 2 * count]
        out_ref, *loaded_refs = rest[2 * count : 2 * count + 3]
        keys, values, scores, weights, bias, query_ref = rest[2 * count + 3 : 2 * count + 9]
        ancestors_ref, tile_of_slot_ref, slot_of, wanted, sems = rest[2 * count + 9 :]
        z, x, y, c = (lax.axis_index(name) for name in AXES)
        sign = 1 - 2 * c
        copies = [
            pltpu.make_async_copy(ancestors_vmem, ancestors_ref, sems.at[0]),
            pltpu.make_async_copy(tile_of_slot_vmem, tile_of_slot_ref, sems.at[1]),
            pltpu.make_async_copy(query_hbm, query_ref, sems.at[2]),
        ]
        for copy in copies:
            copy.start()
        loads = []
        for hops in (2, 1, 3, 0):
            column = pl.multiple_of((lax.rem(y + hops * sign + NY, NY) * 2 + c) * 1024, 1024)
            for source, target in zip(weight_refs, loaded_refs):
                loads.append(
                    pltpu.make_async_copy(
                        source.at[:, pl.ds(column, 1024)], target.at[hops], sems.at[3]
                    )
                )
        for copy in loads:
            copy.start()
        for copy in copies[:2]:
            copy.wait()
        for s in range(TILES):
            slot_of[tile_of_slot_ref[0, s]] = s
        for t in range(2):
            start = t * keys_total
            keys[start : start + TILE] = own_ref[t * TILE : (t + 1) * TILE]
            values[start : start + TILE] = own_ref[256 + t * TILE : 256 + (t + 1) * TILE]
            own_slot = (z * NX + x) * 2 + t
            located = []
            for j in range(ANC):
                tile = ancestors_ref[t, j]
                slot = jnp.where(tile >= 0, slot_of[jnp.maximum(tile, 0)], -1)
                keep = jnp.logical_and(slot >= 0, slot != own_slot)
                for earlier in located:
                    keep = jnp.logical_and(keep, slot != earlier)
                located.append(slot)
                wanted[t * ANC + j] = jnp.where(keep, slot, own_slot)
                bias[t, :, (j + 1) * TILE : (j + 2) * TILE] = jnp.full(
                    (8, TILE), jnp.where(keep, 0.0, -jnp.inf), jnp.float32
                )

        def take(i, carry):
            slot = wanted[i]
            second = slot % 2
            chip = slot // 2
            steps = lax.rem((z - chip // NX) * sign + NZ, NZ)
            hops = lax.rem((x - chip % NX) * sign + NX, NX)
            to = pl.multiple_of((i + 1 + jnp.where(i >= ANC, 1, 0)) * TILE, TILE)

            def put(target, source, row, both):
                start = pl.multiple_of(row + second * TILE, TILE) if both else row
                target[pl.ds(to, TILE)] = source[pl.ds(start, TILE)]

            def from_chip(n, h):
                h_other = (NX - h) % NX
                if n == 0 and h == 0:
                    put(keys, own_ref, 0, True)
                    put(values, own_ref, 256, True)
                elif n in (0, 4):

                    @pl.when(c == 0)
                    def _():
                        put(keys, *spot(mine_refs, n, h, 0))
                        put(values, *spot(theirs_refs, n, h_other, 1))

                    @pl.when(c == 1)
                    def _():
                        put(keys, *spot(theirs_refs, n, h_other, 0))
                        put(values, *spot(mine_refs, n, h, 1))

                elif n < 4:
                    put(keys, *spot(mine_refs, n, h, 0))
                    put(values, *spot(mine_refs, n, h, 1))
                else:
                    put(keys, *spot(theirs_refs, NZ - n, h_other, 0))
                    put(values, *spot(theirs_refs, NZ - n, h_other, 1))

            def branch(case, low, high):
                if high - low == 1:
                    from_chip(low % NZ, low // NZ)
                    return
                middle = (low + high) // 2
                lax.cond(
                    case < middle,
                    lambda: branch(case, low, middle),
                    lambda: branch(case, middle, high),
                )

            branch(hops * NZ + steps, 0, NX * NZ)
            return carry

        lax.fori_loop(0, 2 * ANC, take, 0)
        copies[2].wait()
        rows_id = lax.broadcasted_iota(jnp.int32, (TILE, TILE), 0)
        cols_id = lax.broadcasted_iota(jnp.int32, (TILE, TILE), 1)
        causal = jnp.where(rows_id >= cols_id, 0.0, -jnp.inf)
        for t in range(2):
            q = jnp.concatenate(
                [
                    query_ref[t * TILE : (t + 1) * TILE, h * HEAD : (h + 1) * HEAD]
                    for h in range(GROUP)
                ],
                axis=0,
            )
            scores[t] = lax.dot_general(
                q,
                keys[t * keys_total : (t + 1) * keys_total],
                (((1,), (1,)), ((), ())),
                preferred_element_type=jnp.float32,
            )
        for t in range(2):
            totals = []
            for h in range(GROUP):
                rows = slice(h * TILE, (h + 1) * TILE)
                near = scores[t, rows, :TILE] + causal
                far = scores[t, rows, TILE:] + bias[t, 0:1, TILE:]
                peak = jnp.maximum(
                    jnp.max(near, axis=1, keepdims=True), jnp.max(far, axis=1, keepdims=True)
                )
                near = jnp.exp2((near - peak) * scale)
                far = jnp.exp2((far - peak) * scale)
                totals.append(
                    jnp.sum(near, axis=1, keepdims=True) + jnp.sum(far, axis=1, keepdims=True)
                )
                weights[t, rows, :TILE] = near.astype(jnp.bfloat16)
                weights[t, rows, TILE:] = far.astype(jnp.bfloat16)
            mixed = jnp.dot(
                weights[t],
                values[t * keys_total : (t + 1) * keys_total],
                preferred_element_type=jnp.float32,
            )
            for h in range(GROUP):
                out_ref[t * TILE : (t + 1) * TILE, h * HEAD : (h + 1) * HEAD] = (
                    mixed[h * TILE : (h + 1) * TILE] / totals[h]
                ).astype(jnp.bfloat16)
        for copy in loads:
            copy.wait()

    return pl.pallas_call(
        kernel,
        out_shape=[
            pltpu.VMEM((2 * TILE, GROUP * HEAD), jnp.bfloat16),
            pltpu.VMEM((NY, 512, 1024), jnp.bfloat16),
            pltpu.VMEM((NY, 512, 1024), jnp.bfloat16),
        ],
        in_specs=[pl.BlockSpec(memory_space=pltpu.HBM)] * 3
        + [pl.BlockSpec(memory_space=pltpu.VMEM)] * (3 + 2 * count),
        out_specs=[pl.BlockSpec(memory_space=pltpu.VMEM)] * 3,
        scratch_shapes=[
            pltpu.VMEM((2 * keys_total, HEAD), jnp.bfloat16),
            pltpu.VMEM((2 * keys_total, HEAD), jnp.bfloat16),
            pltpu.VMEM((2, GROUP * TILE, keys_total), jnp.float32),
            pltpu.VMEM((2, GROUP * TILE, keys_total), jnp.bfloat16),
            pltpu.VMEM((2, 8, keys_total), jnp.float32),
            pltpu.VMEM((2 * TILE, GROUP * HEAD), jnp.bfloat16),
            pltpu.SMEM((2, ANC), jnp.int32),
            pltpu.SMEM((1, TILES), jnp.int32),
            pltpu.SMEM((TILES,), jnp.int32),
            pltpu.SMEM((2 * ANC,), jnp.int32),
            pltpu.SemaphoreType.DMA((4,)),
        ],
        compiler_params=pltpu.CompilerParams(vmem_limit_bytes=28 << 20),
        name="attend",
    )(
        *(
            pltpu.with_memory_space_constraint(array, pltpu.HBM)
            for array in (query, weight, weight_other)
        ),
        ancestors,
        tile_of_slot,
        own,
        *mine,
        *theirs,
    )


def project(attended, attended_other, weights, weights_other, parts, added=(), dtype=jnp.bfloat16):
    count = len(parts)
    sizes = [2 * TILE if tile is None else TILE for _, tile in parts]

    def kernel(a_ref, b_ref, w_ref, v_ref, *rest):
        added_refs, out_refs = rest[: len(added)], rest[len(added) :]
        c = lax.axis_index("c")
        for k, ((hops, tile), rows) in enumerate(zip(parts, sizes)):
            row = 0 if tile is None else pl.multiple_of((c if tile == 0 else 1 - c) * TILE, TILE)
            for n in range(0, 1024, 256):
                term = jnp.dot(
                    a_ref[pl.ds(row, rows)],
                    w_ref[hops, :, n : n + 256],
                    preferred_element_type=jnp.float32,
                )
                term += jnp.dot(
                    b_ref[pl.ds(row, rows)],
                    v_ref[hops, :, n : n + 256],
                    preferred_element_type=jnp.float32,
                )
                if added:
                    term += added_refs[k][:, n : n + 256].astype(jnp.float32)
                out_refs[k][:, n : n + 256] = term.astype(dtype)

    return pl.pallas_call(
        kernel,
        out_shape=[jax.ShapeDtypeStruct((rows, 1024), dtype) for rows in sizes],
        in_specs=[pl.BlockSpec(memory_space=pltpu.VMEM)] * (4 + len(added)),
        out_specs=[pl.BlockSpec(memory_space=pltpu.VMEM)] * count,
        compiler_params=pltpu.CompilerParams(vmem_limit_bytes=16 << 20),
        name="project",
    )(attended, attended_other, weights, weights_other, *added)


def finish(here, from_back0, from_ahead0, from_ahead1, from_back1, residual):
    def kernel(here_ref, b0_ref, a0_ref, a1_ref, b1_ref, residual_ref, hidden_ref, sums_ref):
        c = lax.axis_index("c")
        ones = jnp.ones((8, 128), jnp.float32)
        for tile, first_ref, second_ref in ((c, b0_ref, a0_ref), (1 - c, a1_ref, b1_ref)):
            row = pl.multiple_of(tile * TILE, TILE)
            squares = jnp.zeros((TILE, 128), jnp.float32)
            for n in range(0, 1024, 128):
                columns = slice(n, n + 128)
                share = first_ref[:, columns].astype(jnp.float32)
                share += second_ref[:, columns].astype(jnp.float32)
                share += here_ref[pl.ds(row, TILE), columns]
                share += residual_ref[pl.ds(row, TILE), columns].astype(jnp.float32)
                hidden = share.astype(jnp.bfloat16)
                hidden_ref[pl.ds(row, TILE), columns] = hidden
                hidden = hidden.astype(jnp.float32)
                squares += hidden * hidden
            sums = lax.dot_general(
                ones,
                squares,
                (((1,), (1,)), ((), ())),
                precision=lax.Precision.HIGHEST,
                preferred_element_type=jnp.float32,
            )
            for k in range(NY * NC):
                sums_ref[k, :, pl.ds(row, TILE)] = sums[0:1]

    return pl.pallas_call(
        kernel,
        out_shape=[
            pltpu.VMEM((2 * TILE, 1024), jnp.bfloat16),
            pltpu.VMEM((NY * NC, 1, 2 * TILE), jnp.float32),
        ],
        in_specs=[pl.BlockSpec(memory_space=pltpu.VMEM)] * 6,
        out_specs=[pl.BlockSpec(memory_space=pltpu.VMEM)] * 2,
        compiler_params=pltpu.CompilerParams(vmem_limit_bytes=8 << 20),
        name="finish",
    )(here, from_back0, from_ahead0, from_ahead1, from_back1, residual)


def normalize(hidden, sums, gain):
    def kernel(hidden_ref, sums_ref, gain_ref, hidden_hbm, normed_hbm, normed_ref, sems):
        out = pltpu.make_async_copy(hidden_ref, hidden_hbm, sems.at[0])
        out.start()
        copies = []
        for tile in range(2):
            rows = slice(tile * TILE, (tile + 1) * TILE)
            total = sums_ref[0, :, rows]
            for k in range(1, NY * NC):
                total += sums_ref[k, :, rows]
            scale = lax.rsqrt(jnp.broadcast_to(total, (TILE, TILE)) / D + 1e-05)
            scale = jnp.transpose(scale)
            for n in range(0, 1024, 128):
                columns = slice(n, n + 128)
                normed_ref[rows, columns] = (
                    hidden_ref[rows, columns].astype(jnp.float32) * scale * gain_ref[:, columns]
                ).astype(jnp.bfloat16)
            copies.append(
                pltpu.make_async_copy(normed_ref.at[rows], normed_hbm.at[rows], sems.at[1 + tile])
            )
            copies[-1].start()
        out.wait()
        for copy in copies:
            copy.wait()

    shape = jax.ShapeDtypeStruct((2 * TILE, 1024), jnp.bfloat16)
    return pl.pallas_call(
        kernel,
        out_shape=[shape, shape],
        in_specs=[pl.BlockSpec(memory_space=pltpu.VMEM)] * 3,
        out_specs=[pl.BlockSpec(memory_space=pltpu.HBM)] * 2,
        scratch_shapes=[
            pltpu.VMEM((2 * TILE, 1024), jnp.bfloat16),
            pltpu.SemaphoreType.DMA((3,)),
        ],
        compiler_params=pltpu.CompilerParams(vmem_limit_bytes=8 << 20),
        name="normalize",
    )(hidden, sums, gain.reshape(1, 1024))


def layer(query, keys_values, ancestors, tile_of_slot, residual, norm_gain, out_weight):
    own, own_half, anc_here, tiles_here = pick(keys_values, ancestors, tile_of_slot)
    own = own.reshape(BLOCK, HEAD)
    weight_other = other_core(out_weight)
    mine, theirs = gather_pairs(own, own_half, ancestors, tiles_here)
    attended, *weights = attend(
        query, own, mine, theirs, anc_here, tiles_here, out_weight, weight_other
    )
    args = (attended, other_core(attended), *weights)
    (across0,) = project(*args, [(2, 0)])
    relay_ahead = along_y(across0, 1)
    (across1,) = project(*args, [(2, 1)])
    relay_back = along_y(across1, -1)
    direct1, direct0 = project(*args, [(1, 1), (3, 0)])
    from_back1 = along_y(direct1, 1)
    from_ahead0 = along_y(direct0, -1)
    (joined0,) = project(*args, [(1, 0)], (relay_ahead,))
    from_back0 = along_y(joined0, 1)
    (joined1,) = project(*args, [(3, 1)], (relay_back,))
    from_ahead1 = along_y(joined1, -1)
    (here,) = project(*args, [(0, None)], (), jnp.float32)
    hidden, sums = finish(here, from_back0, from_ahead0, from_ahead1, from_back1, residual)
    sums = lax.all_to_all(sums, ("y", "c"), 0, 0, tiled=True)
    return tuple(normalize(hidden, sums, norm_gain))


def solution(mesh):
    fine = Mesh(mesh.devices.reshape(NZ, NX, NY, NC), AXES)
    rows, columns = ("z", "x"), ("y", "c")
    return jax.shard_map(
        layer,
        mesh=fine,
        in_specs=(
            P(rows, columns),
            P(None, rows, None),
            P(rows, None),
            P(),
            P(rows, columns),
            P(columns),
            P(columns, None),
        ),
        out_specs=(P(rows, columns), P(rows, columns)),
        check_vma=False,
    )
```

```python
import jax
import jax.numpy as jnp
from jax import lax
from jax.experimental import pallas as pl
from jax.experimental.pallas import tpu as pltpu
from jax.sharding import Mesh, PartitionSpec as P


D = 8192
HEAD = 128
TILE = 128
ANC = 12
NZ, NX, NY, NC = 8, 4, 4, 2
TILES = 64
BLOCK = 512
GROUP = 4
LOG2E = 1.4426950408889634
AXES = ("z", "x", "y", "c")


def permutation(target):
    pairs = []
    for z in range(NZ):
        for x in range(NX):
            for y in range(NY):
                for c in range(NC):
                    tz, tx, ty, tc = target(z, x, y, c)
                    source = ((z * NX + x) * NY + y) * NC + c
                    pairs.append(
                        (source, (((tz % NZ) * NX + tx % NX) * NY + ty % NY) * NC + tc % NC)
                    )
    return pairs


def along_z(array, hops):
    return lax.ppermute(
        array, AXES, permutation(lambda z, x, y, c: (z + hops * (1 - 2 * c), x, y, c))
    )


def along_x(array, hops):
    return lax.ppermute(
        array, AXES, permutation(lambda z, x, y, c: (z, x + hops * (1 - 2 * c), y, c))
    )


def along_y(array, hops):
    return lax.ppermute(
        array, AXES, permutation(lambda z, x, y, c: (z, x, y + hops * (1 - 2 * c), c))
    )


def other_core(array):
    return lax.ppermute(array, AXES, permutation(lambda z, x, y, c: (z, x, y, c + 1)))


def choose(ancestors, tile_of_slot):
    def kernel(first_ref, second_ref, third_ref, tile_of_slot_ref, out_ref):
        z, x, c = (lax.axis_index(name) for name in ("z", "x", "c"))
        sign = 1 - 2 * c
        slots = lax.broadcasted_iota(jnp.int32, (1, TILES), 1)
        for n in range(NZ):
            slot = (lax.rem(z - n * sign + NZ, NZ) * NX + x) * 2 + 1
            tile = jnp.sum(
                jnp.where(slots == slot, tile_of_slot_ref[...], 0), axis=1, keepdims=True
            )
            for k, ref in enumerate((first_ref, second_ref, third_ref)):
                named = jnp.where(ref[...] == tile, 1.0, 0.0)
                named = jnp.max(jnp.max(named, axis=1, keepdims=True), axis=0, keepdims=True)
                out_ref[k * NZ + n : k * NZ + n + 1, :] = jnp.broadcast_to(named, (1, 128))

    return pl.pallas_call(
        kernel,
        out_shape=pltpu.VMEM((3 * NZ, 128), jnp.float32),
        in_specs=[pl.BlockSpec(memory_space=pltpu.VMEM)] * 4,
        out_specs=pl.BlockSpec(memory_space=pltpu.VMEM),
        compiler_params=pltpu.CompilerParams(vmem_limit_bytes=4 << 20),
        name="choose",
    )(*ancestors, tile_of_slot)


def select(chosen, arrays, steps):
    total = sum(array.shape[0] for array in arrays) // 2

    def kernel(chosen_ref, *refs):
        array_refs, out_refs = refs[: len(arrays)], refs[len(arrays) :]
        for k, out_ref in enumerate(out_refs):
            to = 0
            for ref, n in zip(array_refs, steps):
                second = chosen_ref[k * NZ + n : k * NZ + n + 1, :]
                first = jnp.broadcast_to(1.0 - second, (TILE, 128)).astype(jnp.bfloat16)
                second = jnp.broadcast_to(second, (TILE, 128)).astype(jnp.bfloat16)
                for row in range(0, ref.shape[0], 2 * TILE):
                    out_ref[to : to + TILE] = (
                        ref[row : row + TILE] * first + ref[row + TILE : row + 2 * TILE] * second
                    )
                    to += TILE

    return pl.pallas_call(
        kernel,
        out_shape=[pltpu.VMEM((total, HEAD), jnp.bfloat16)] * 3,
        in_specs=[pl.BlockSpec(memory_space=pltpu.VMEM)] * (1 + len(arrays)),
        out_specs=[pl.BlockSpec(memory_space=pltpu.VMEM)] * 3,
        compiler_params=pltpu.CompilerParams(vmem_limit_bytes=4 << 20),
        name="select",
    )(chosen, *arrays)


def gather_pairs(own, own_half, ancestors, tile_of_slot):
    asked_ahead = along_x(ancestors, -1)
    asked_back = other_core(asked_ahead)
    asked_across = along_x(ancestors, 2)
    near1 = along_z(own, 1)
    near2 = along_z(own, 2)
    near3 = along_z(near1, 2)
    half4 = along_z(lax.dynamic_slice_in_dim(near2, lax.axis_index("c") * 256, 256, 0), 2)
    chosen = choose((asked_ahead, asked_back, asked_across), tile_of_slot)
    arrays = [near1, near2, near3, half4]
    for parts, steps in (((own_half, near1, near2), (0, 1, 2)), ((near3, half4), (3, 4))):
        messages = select(chosen, parts, steps)
        for hops, message in reversed(tuple(zip((1, -1, 2), messages))):
            arrays.append(along_x(message, hops))
    theirs = []
    for array in arrays:
        theirs.append(other_core(array))
    return arrays, theirs


def pick(keys_values, ancestors, tile_of_slot):
    def kernel(all_ref, anc_hbm, tiles_hbm, block_ref, half_ref, anc_ref, tiles_ref, sems):
        y, c = lax.axis_index("y"), lax.axis_index("c")
        head = all_ref.at[:, :, pl.ds(pl.multiple_of(y * HEAD, HEAD), HEAD)]
        copies = [
            pltpu.make_async_copy(head, block_ref, sems.at[0]),
            pltpu.make_async_copy(head.at[c], half_ref, sems.at[1]),
            pltpu.make_async_copy(anc_hbm, anc_ref, sems.at[2]),
            pltpu.make_async_copy(tiles_hbm, tiles_ref, sems.at[3]),
        ]
        for copy in copies:
            copy.start()
        for copy in copies:
            copy.wait()

    return pl.pallas_call(
        kernel,
        out_shape=[
            pltpu.VMEM((2, 256, HEAD), jnp.bfloat16),
            pltpu.VMEM((256, HEAD), jnp.bfloat16),
            pltpu.VMEM((2, ANC), jnp.int32),
            pltpu.VMEM((1, TILES), jnp.int32),
        ],
        in_specs=[pl.BlockSpec(memory_space=pltpu.HBM)] * 3,
        out_specs=[pl.BlockSpec(memory_space=pltpu.VMEM)] * 4,
        scratch_shapes=[pltpu.SemaphoreType.DMA((4,))],
        compiler_params=pltpu.CompilerParams(vmem_limit_bytes=4 << 20),
        name="pick",
    )(
        *(
            pltpu.with_memory_space_constraint(array, pltpu.HBM)
            for array in (keys_values, ancestors, tile_of_slot.reshape(1, TILES))
        )
    )


def spot(refs, steps, hops, part):
    whole, (across1, back1, ahead1, across2, back2, ahead2) = refs[:4], refs[4:]
    if hops == 0:
        return whole[steps - 1], (0 if steps == 4 else 256 * part), True
    row = {0: 0, 1: 128, 2: 384, 3: 0, 4: 256}[steps] + (0 if steps in (0, 4) else 128 * part)
    first, second = {1: (ahead1, ahead2), 3: (back1, back2), 2: (across1, across2)}[hops]
    return (first if steps < 3 else second), row, False


def attend(query, own, mine, theirs, ancestors, tile_of_slot, weight, weight_other):
    scale = HEAD**-0.5 * LOG2E
    keys_total = (ANC + 1) * TILE
    count = len(mine)

    def kernel(query_hbm, *rest):
        weight_refs, rest = rest[:2], rest[2:]
        (ancestors_vmem, tile_of_slot_vmem, own_ref), rest = rest[:3], rest[3:]
        mine_refs, theirs_refs = rest[:count], rest[count : 2 * count]
        out_ref, *loaded_refs = rest[2 * count : 2 * count + 3]
        keys, values, scores, weights, bias, query_ref = rest[2 * count + 3 : 2 * count + 9]
        ancestors_ref, tile_of_slot_ref, slot_of, wanted, sems = rest[2 * count + 9 :]
        z, x, y, c = (lax.axis_index(name) for name in AXES)
        sign = 1 - 2 * c
        copies = [
            pltpu.make_async_copy(ancestors_vmem, ancestors_ref, sems.at[0]),
            pltpu.make_async_copy(tile_of_slot_vmem, tile_of_slot_ref, sems.at[1]),
            pltpu.make_async_copy(query_hbm, query_ref, sems.at[2]),
        ]
        for copy in copies:
            copy.start()
        loads = []
        for hops in (2, 1, 3, 0):
            column = pl.multiple_of((lax.rem(y + hops * sign + NY, NY) * 2 + c) * 1024, 1024)
            for source, target in zip(weight_refs, loaded_refs):
                loads.append(
                    pltpu.make_async_copy(
                        source.at[:, pl.ds(column, 1024)], target.at[hops], sems.at[3]
                    )
                )
        for copy in loads:
            copy.start()
        for copy in copies[:2]:
            copy.wait()
        for s in range(TILES):
            slot_of[tile_of_slot_ref[0, s]] = s
        for t in range(2):
            start = t * keys_total
            keys[start : start + TILE] = own_ref[t * TILE : (t + 1) * TILE]
            values[start : start + TILE] = own_ref[256 + t * TILE : 256 + (t + 1) * TILE]
            own_slot = (z * NX + x) * 2 + t
            located = []
            for j in range(ANC):
                tile = ancestors_ref[t, j]
                slot = jnp.where(tile >= 0, slot_of[jnp.maximum(tile, 0)], -1)
                keep = jnp.logical_and(slot >= 0, slot != own_slot)
                for earlier in located:
                    keep = jnp.logical_and(keep, slot != earlier)
                located.append(slot)
                wanted[t * ANC + j] = jnp.where(keep, slot, own_slot)
                bias[t, :, (j + 1) * TILE : (j + 2) * TILE] = jnp.full(
                    (8, TILE), jnp.where(keep, 0.0, -jnp.inf), jnp.float32
                )

        def take(i, carry):
            slot = wanted[i]
            second = slot % 2
            chip = slot // 2
            steps = lax.rem((z - chip // NX) * sign + NZ, NZ)
            hops = lax.rem((x - chip % NX) * sign + NX, NX)
            to = pl.multiple_of((i + 1 + jnp.where(i >= ANC, 1, 0)) * TILE, TILE)

            def put(target, source, row, both):
                start = pl.multiple_of(row + second * TILE, TILE) if both else row
                target[pl.ds(to, TILE)] = source[pl.ds(start, TILE)]

            def from_chip(n, h):
                h_other = (NX - h) % NX
                if n == 0 and h == 0:
                    put(keys, own_ref, 0, True)
                    put(values, own_ref, 256, True)
                elif n in (0, 4):

                    @pl.when(c == 0)
                    def _():
                        put(keys, *spot(mine_refs, n, h, 0))
                        put(values, *spot(theirs_refs, n, h_other, 1))

                    @pl.when(c == 1)
                    def _():
                        put(keys, *spot(theirs_refs, n, h_other, 0))
                        put(values, *spot(mine_refs, n, h, 1))

                elif n < 4:
                    put(keys, *spot(mine_refs, n, h, 0))
                    put(values, *spot(mine_refs, n, h, 1))
                else:
                    put(keys, *spot(theirs_refs, NZ - n, h_other, 0))
                    put(values, *spot(theirs_refs, NZ - n, h_other, 1))

            def branch(case, low, high):
                if high - low == 1:
                    from_chip(low % NZ, low // NZ)
                    return
                middle = (low + high) // 2
                lax.cond(
                    case < middle,
                    lambda: branch(case, low, middle),
                    lambda: branch(case, middle, high),
                )

            branch(hops * NZ + steps, 0, NX * NZ)
            return carry

        lax.fori_loop(0, 2 * ANC, take, 0)
        copies[2].wait()
        rows_id = lax.broadcasted_iota(jnp.int32, (TILE, TILE), 0)
        cols_id = lax.broadcasted_iota(jnp.int32, (TILE, TILE), 1)
        causal = jnp.where(rows_id >= cols_id, 0.0, -jnp.inf)
        for t in range(2):
            q = jnp.concatenate(
                [
                    query_ref[t * TILE : (t + 1) * TILE, h * HEAD : (h + 1) * HEAD]
                    for h in range(GROUP)
                ],
                axis=0,
            )
            scores[t] = lax.dot_general(
                q,
                keys[t * keys_total : (t + 1) * keys_total],
                (((1,), (1,)), ((), ())),
                preferred_element_type=jnp.float32,
            )
        for t in range(2):
            totals = []
            for h in range(GROUP):
                rows = slice(h * TILE, (h + 1) * TILE)
                near = scores[t, rows, :TILE] + causal
                far = scores[t, rows, TILE:] + bias[t, 0:1, TILE:]
                peak = jnp.maximum(
                    jnp.max(near, axis=1, keepdims=True), jnp.max(far, axis=1, keepdims=True)
                )
                near = jnp.exp2((near - peak) * scale)
                far = jnp.exp2((far - peak) * scale)
                totals.append(
                    jnp.sum(near, axis=1, keepdims=True) + jnp.sum(far, axis=1, keepdims=True)
                )
                weights[t, rows, :TILE] = near.astype(jnp.bfloat16)
                weights[t, rows, TILE:] = far.astype(jnp.bfloat16)
            mixed = jnp.dot(
                weights[t],
                values[t * keys_total : (t + 1) * keys_total],
                preferred_element_type=jnp.float32,
            )
            for h in range(GROUP):
                out_ref[t * TILE : (t + 1) * TILE, h * HEAD : (h + 1) * HEAD] = (
                    mixed[h * TILE : (h + 1) * TILE] / totals[h]
                ).astype(jnp.bfloat16)
        for copy in loads:
            copy.wait()

    return pl.pallas_call(
        kernel,
        out_shape=[
            pltpu.VMEM((2 * TILE, GROUP * HEAD), jnp.bfloat16),
            pltpu.VMEM((NY, 512, 1024), jnp.bfloat16),
            pltpu.VMEM((NY, 512, 1024), jnp.bfloat16),
        ],
        in_specs=[pl.BlockSpec(memory_space=pltpu.HBM)] * 3
        + [pl.BlockSpec(memory_space=pltpu.VMEM)] * (3 + 2 * count),
        out_specs=[pl.BlockSpec(memory_space=pltpu.VMEM)] * 3,
        scratch_shapes=[
            pltpu.VMEM((2 * keys_total, HEAD), jnp.bfloat16),
            pltpu.VMEM((2 * keys_total, HEAD), jnp.bfloat16),
            pltpu.VMEM((2, GROUP * TILE, keys_total), jnp.float32),
            pltpu.VMEM((2, GROUP * TILE, keys_total), jnp.bfloat16),
            pltpu.VMEM((2, 8, keys_total), jnp.float32),
            pltpu.VMEM((2 * TILE, GROUP * HEAD), jnp.bfloat16),
            pltpu.SMEM((2, ANC), jnp.int32),
            pltpu.SMEM((1, TILES), jnp.int32),
            pltpu.SMEM((TILES,), jnp.int32),
            pltpu.SMEM((2 * ANC,), jnp.int32),
            pltpu.SemaphoreType.DMA((4,)),
        ],
        compiler_params=pltpu.CompilerParams(vmem_limit_bytes=28 << 20),
        name="attend",
    )(
        *(
            pltpu.with_memory_space_constraint(array, pltpu.HBM)
            for array in (query, weight, weight_other)
        ),
        ancestors,
        tile_of_slot,
        own,
        *mine,
        *theirs,
    )


def project(attended, attended_other, weights, weights_other, parts, added=(), dtype=jnp.bfloat16):
    count = len(parts)
    sizes = [2 * TILE if tile is None else TILE for _, tile in parts]

    def kernel(a_ref, b_ref, w_ref, v_ref, *rest):
        added_refs, out_refs = rest[: len(added)], rest[len(added) :]
        c = lax.axis_index("c")
        for k, ((hops, tile), rows) in enumerate(zip(parts, sizes)):
            row = 0 if tile is None else pl.multiple_of((c if tile == 0 else 1 - c) * TILE, TILE)
            for n in range(0, 1024, 256):
                term = jnp.dot(
                    a_ref[pl.ds(row, rows)],
                    w_ref[hops, :, n : n + 256],
                    preferred_element_type=jnp.float32,
                )
                term += jnp.dot(
                    b_ref[pl.ds(row, rows)],
                    v_ref[hops, :, n : n + 256],
                    preferred_element_type=jnp.float32,
                )
                if added:
                    term += added_refs[k][:, n : n + 256].astype(jnp.float32)
                out_refs[k][:, n : n + 256] = term.astype(dtype)

    return pl.pallas_call(
        kernel,
        out_shape=[jax.ShapeDtypeStruct((rows, 1024), dtype) for rows in sizes],
        in_specs=[pl.BlockSpec(memory_space=pltpu.VMEM)] * (4 + len(added)),
        out_specs=[pl.BlockSpec(memory_space=pltpu.VMEM)] * count,
        compiler_params=pltpu.CompilerParams(vmem_limit_bytes=16 << 20),
        name="project",
    )(attended, attended_other, weights, weights_other, *added)


def finish(here, from_back0, from_ahead0, from_ahead1, from_back1, residual):
    def kernel(here_ref, b0_ref, a0_ref, a1_ref, b1_ref, residual_ref, hidden_ref, sums_ref):
        c = lax.axis_index("c")
        ones = jnp.ones((8, 128), jnp.float32)
        for tile, first_ref, second_ref in ((c, b0_ref, a0_ref), (1 - c, a1_ref, b1_ref)):
            row = pl.multiple_of(tile * TILE, TILE)
            squares = jnp.zeros((TILE, 128), jnp.float32)
            for n in range(0, 1024, 128):
                columns = slice(n, n + 128)
                share = first_ref[:, columns].astype(jnp.float32)
                share += second_ref[:, columns].astype(jnp.float32)
                share += here_ref[pl.ds(row, TILE), columns]
                share += residual_ref[pl.ds(row, TILE), columns].astype(jnp.float32)
                hidden = share.astype(jnp.bfloat16)
                hidden_ref[pl.ds(row, TILE), columns] = hidden
                hidden = hidden.astype(jnp.float32)
                squares += hidden * hidden
            sums = lax.dot_general(
                ones,
                squares,
                (((1,), (1,)), ((), ())),
                precision=lax.Precision.HIGHEST,
                preferred_element_type=jnp.float32,
            )
            for k in range(NY * NC):
                sums_ref[k, :, pl.ds(row, TILE)] = sums[0:1]

    return pl.pallas_call(
        kernel,
        out_shape=[
            pltpu.VMEM((2 * TILE, 1024), jnp.bfloat16),
            pltpu.VMEM((NY * NC, 1, 2 * TILE), jnp.float32),
        ],
        in_specs=[pl.BlockSpec(memory_space=pltpu.VMEM)] * 6,
        out_specs=[pl.BlockSpec(memory_space=pltpu.VMEM)] * 2,
        compiler_params=pltpu.CompilerParams(vmem_limit_bytes=8 << 20),
        name="finish",
    )(here, from_back0, from_ahead0, from_ahead1, from_back1, residual)


def normalize(hidden, sums, gain):
    def kernel(hidden_ref, sums_ref, gain_ref, hidden_hbm, normed_hbm, normed_ref, sems):
        out = pltpu.make_async_copy(hidden_ref, hidden_hbm, sems.at[0])
        out.start()
        copies = []
        for tile in range(2):
            rows = slice(tile * TILE, (tile + 1) * TILE)
            total = sums_ref[0, :, rows]
            for k in range(1, NY * NC):
                total += sums_ref[k, :, rows]
            scale = lax.rsqrt(jnp.broadcast_to(total, (TILE, TILE)) / D + 1e-05)
            scale = jnp.transpose(scale)
            for n in range(0, 1024, 128):
                columns = slice(n, n + 128)
                normed_ref[rows, columns] = (
                    hidden_ref[rows, columns].astype(jnp.float32) * scale * gain_ref[:, columns]
                ).astype(jnp.bfloat16)
            copies.append(
                pltpu.make_async_copy(normed_ref.at[rows], normed_hbm.at[rows], sems.at[1 + tile])
            )
            copies[-1].start()
        out.wait()
        for copy in copies:
            copy.wait()

    shape = jax.ShapeDtypeStruct((2 * TILE, 1024), jnp.bfloat16)
    return pl.pallas_call(
        kernel,
        out_shape=[shape, shape],
        in_specs=[pl.BlockSpec(memory_space=pltpu.VMEM)] * 3,
        out_specs=[pl.BlockSpec(memory_space=pltpu.HBM)] * 2,
        scratch_shapes=[
            pltpu.VMEM((2 * TILE, 1024), jnp.bfloat16),
            pltpu.SemaphoreType.DMA((3,)),
        ],
        compiler_params=pltpu.CompilerParams(vmem_limit_bytes=8 << 20),
        name="normalize",
    )(hidden, sums, gain.reshape(1, 1024))


def layer(query, keys_values, ancestors, tile_of_slot, residual, norm_gain, out_weight):
    own, own_half, anc_here, tiles_here = pick(keys_values, ancestors, tile_of_slot)
    own = own.reshape(BLOCK, HEAD)
    weight_other = other_core(out_weight)
    mine, theirs = gather_pairs(own, own_half, ancestors, tiles_here)
    attended, *weights = attend(
        query, own, mine, theirs, anc_here, tiles_here, out_weight, weight_other
    )
    args = (attended, other_core(attended), *weights)
    (across0,) = project(*args, [(2, 0)])
    relay_ahead = along_y(across0, 1)
    (across1,) = project(*args, [(2, 1)])
    relay_back = along_y(across1, -1)
    (direct1,) = project(*args, [(1, 1)])
    from_back1 = along_y(direct1, 1)
    (direct0,) = project(*args, [(3, 0)])
    from_ahead0 = along_y(direct0, -1)
    (joined0,) = project(*args, [(1, 0)], (relay_ahead,))
    from_back0 = along_y(joined0, 1)
    (joined1,) = project(*args, [(3, 1)], (relay_back,))
    from_ahead1 = along_y(joined1, -1)
    (here,) = project(*args, [(0, None)], (), jnp.float32)
    hidden, sums = finish(here, from_back0, from_ahead0, from_ahead1, from_back1, residual)
    sums = lax.all_to_all(sums, ("y", "c"), 0, 0, tiled=True)
    return tuple(normalize(hidden, sums, norm_gain))


def solution(mesh):
    fine = Mesh(mesh.devices.reshape(NZ, NX, NY, NC), AXES)
    rows, columns = ("z", "x"), ("y", "c")
    return jax.shard_map(
        layer,
        mesh=fine,
        in_specs=(
            P(rows, columns),
            P(None, rows, None),
            P(rows, None),
            P(),
            P(rows, columns),
            P(columns),
            P(columns, None),
        ),
        out_specs=(P(rows, columns), P(rows, columns)),
        check_vma=False,
    )
```
